512 devices in a mesh: fsdp: 32 (over x, y_hi, core), tensor: 16 (over z, y_lo).
Axes of the slice: x: 4, y: 8 (y_hi: 4, y_lo: 2; y = y_hi * 2 + y_lo), z: 8, core: 2. Of those that a mesh axis runs over, the one named last changes fastest.
Arguments:
- policy_token_inputs: bfloat16 [6144, 8192], P('fsdp', 'tensor'), may hold values from -6 to 6
- reference_tokens: bfloat16 [6144, 8192], P('fsdp', 'tensor'), may hold values from -6 to 6
- cotangent: bfloat16 [6144, 4096], P('fsdp', 'tensor'), may hold values from -6 to 6
- query_weight: bfloat16 [8192, 4096], P('fsdp', 'tensor'), may hold values from -1 to 1
- key_weight: bfloat16 [8192, 512], P('fsdp', 'tensor'), may hold values from -1 to 1
- value_weight: bfloat16 [8192, 512], P('fsdp', 'tensor'), may hold values from -0.0625 to 0.0625
- query_down: bfloat16 [8192, 64], P('tensor'), may hold values from -0.0625 to 0.0625
- value_down: bfloat16 [8192, 64], P('tensor'), may hold values from -0.0625 to 0.0625
- query_raise_factor: bfloat16 [64, 4096], P(None, 'tensor'), may hold values from -0.75 to 0.75
- value_raise_factor: bfloat16 [64, 512], P(None, 'tensor'), may hold values from -0.75 to 0.75
- policy_lengths: int32 [64], P('fsdp'), may hold values from 24 to 96
- reference_lengths: int32 [64], P('fsdp'), may hold values from 24 to 96
- chosen_flags: int32 [64], P('fsdp'), may hold values from 0 to 1, as said below
- log_ratios: float32 [64], P('fsdp'), may hold values from -60 to 60
Outputs:
- reference_context: bfloat16 [6144, 4096], P('fsdp', 'tensor')
- query_down_gradient: float32 [8192, 64], P('tensor')
- value_down_gradient: float32 [8192, 64], P('tensor')
- query_up_gradient: float32 [64, 4096], P(None, 'tensor')
- value_up_gradient: float32 [64, 512], P(None, 'tensor')
The draws below stay inside these ranges and needn't reach their ends.
Inputs may be any that keep to these rules, and one draw needn't show every extreme that they name: `chosen_flags`: sequences 2p and 2p+1 form a pair: one is 1 and the other 0. `policy_lengths`: valid tokens stand at the start of each sequence. `reference_lengths`: valid tokens stand at the start of each sequence.
All inputs are finite; a program needn't handle non-finite values.
Results may differ from the reference program's by a relative error of at most 0.007.
The reference program's roundings to bfloat16 on the way count: a program that leaves them out, or rounds other values in their place, can miss the bound.
Values may be sent and summed in bfloat16 or wider, within the bound.
A program may use at most 64 MiB of HBM per device.

```python
import math
import jax
import jax.numpy as jnp
from jax import lax

D = 8192
HD = 128
HEADS = 32
KVH = 4
RANK = 64
SEQ = 96
NSEQ = 64
TOKENS = 6144


def draw_chosen_flags(key, part):
    chosen_first = jax.random.randint(key, (NSEQ // 2,), 0, 2)
    return jnp.stack([chosen_first, 1 - chosen_first], axis=1).reshape(NSEQ).astype(jnp.int32)


def token_block(key, salt):
    own_key = jax.random.fold_in(key, salt)
    block = jnp.clip(jax.random.normal(jax.random.fold_in(own_key, 1), (TOKENS, D), jnp.float32), -6.0, 6.0)
    return block.astype(jnp.bfloat16)


def draw_policy_token_inputs(key, part):
    return token_block(key, 101)


def draw_reference_tokens(key, part):
    return token_block(key, 202)


def draw_query_weight(key, part):
    own_key = jax.random.fold_in(key, 303)
    base = jnp.clip(jax.random.normal(own_key, (D, HEADS * HD), jnp.float32), -6.0, 6.0) * D ** (-0.5)
    return base.astype(jnp.bfloat16)


def draw_key_weight(key, part):
    own_key = jax.random.fold_in(key, 404)
    base = jnp.clip(jax.random.normal(own_key, (D, KVH * HD), jnp.float32), -6.0, 6.0) * D ** (-0.5)
    return base.astype(jnp.bfloat16)


def place_ends(array, key, low, high):
    longest = array.shape.index(max(array.shape))
    spots = []
    for shift in (0, 1):
        where = [jax.random.randint(jax.random.fold_in(key, axis), (), 0, length) for axis, length in enumerate(array.shape)]
        where[longest] = (where[longest] + shift) % array.shape[longest]
        spots.append(tuple(where))
    return array.at[spots[0]].set(low).at[spots[1]].set(high)


def shard_levels(key, shape, pieces, smallest, largest):
    def one(dim, blocks):
        heights = jax.random.uniform(jax.random.fold_in(jax.random.fold_in(key, 6), dim), (blocks,), jnp.float32, smallest / len(pieces), largest / len(pieces))
        return jnp.repeat(jnp.exp(heights), shape[dim] // blocks).reshape((-1,) + (1,) * (len(shape) - dim - 1))

    level = one(*pieces[0])
    for cut in pieces[1:]:
        level = level * one(*cut)
    return level


def normal_values(stream_key, dims, spread, limit, cuts=(), held_as=jnp.bfloat16):
    drawn = jax.random.normal(stream_key, dims, jnp.float32) * spread
    if len(cuts) > 0:
        drawn = shard_levels(stream_key, dims, cuts, -0.22, 0.18) * drawn
    return jnp.clip(drawn, min=-limit, max=limit).astype(held_as)


def setup_inputs(seed: int = 0) -> dict:
    splits = jax.random.split(jax.random.key(seed), 15)
    policy_token_inputs = draw_policy_token_inputs(jax.random.fold_in(splits[14], 71), 0)
    reference_tokens = draw_reference_tokens(jax.random.fold_in(splits[14], 71), 0)
    cotangent = normal_values(splits[2], (TOKENS, HEADS * HD), 1.0, 6.0, ((0, 32), (1, 16)))
    query_weight = draw_query_weight(jax.random.fold_in(splits[14], 71), 0)
    key_weight = draw_key_weight(jax.random.fold_in(splits[14], 71), 0)
    value_weight = normal_values(splits[5], (D, KVH * HD), D ** -0.5, 0.0625, ((0, 32), (1, 16)))
    query_down = normal_values(splits[6], (D, RANK), D ** -0.5, 0.0625, ((0, 16),))
    value_down = normal_values(splits[7], (D, RANK), D ** -0.5, 0.0625, ((0, 16),))
    query_raise_factor = normal_values(splits[8], (RANK, HEADS * HD), RANK ** -0.5, 0.75, ((1, 16),))
    value_raise_factor = normal_values(splits[9], (RANK, KVH * HD), RANK ** -0.5, 0.75, ((1, 16),))
    policy_lengths = place_ends(jax.random.randint(splits[10], (NSEQ,), SEQ // 4, SEQ + 1), jax.random.fold_in(splits[10], 1), SEQ // 4, SEQ).astype(jnp.int32)
    reference_lengths = place_ends(jax.random.randint(splits[11], (NSEQ,), SEQ // 4, SEQ + 1), jax.random.fold_in(splits[11], 1), SEQ // 4, SEQ).astype(jnp.int32)
    chosen_flags = draw_chosen_flags(jax.random.fold_in(splits[14], 71), 0)
    log_ratios = normal_values(splits[13], (NSEQ,), 10.0, 60.0, ((0, 32),), jnp.float32)
    return dict(policy_token_inputs=policy_token_inputs, reference_tokens=reference_tokens, cotangent=cotangent, query_weight=query_weight, key_weight=key_weight, value_weight=value_weight, query_down=query_down, value_down=value_down, query_raise_factor=query_raise_factor, value_raise_factor=value_raise_factor, policy_lengths=policy_lengths, reference_lengths=reference_lengths, chosen_flags=chosen_flags, log_ratios=log_ratios)


ADAPTER_SCALE = 2.0
DPO_BETA = 0.1
MASKED = -1e+30

def angles(length, head_dim):
    position = jnp.arange(length).astype(jnp.float32)
    inverse = 500000.0 ** (-(jnp.arange(head_dim // 2).astype(jnp.float32) * 2.0) / head_dim)
    phase_table = position[:, None] * inverse[None, :]
    return (jnp.cos(phase_table), jnp.sin(phase_table))

def rotate(values_in, cosine, sine_table, direction):
    half_dim = values_in.shape[-1] // 2
    first_half = values_in[..., :half_dim]
    second_half = values_in[..., half_dim:]
    return jnp.concatenate([first_half * cosine - direction * second_half * sine_table, second_half * cosine + direction * first_half * sine_table], axis=-1)

def project_rows(tokens, weight):
    return jnp.dot(tokens, weight, preferred_element_type=jnp.float32)

def reference(policy_token_inputs, reference_tokens, cotangent, query_weight, key_weight, value_weight, query_down, value_down, query_raise_factor, value_raise_factor, policy_lengths, reference_lengths, chosen_flags, log_ratios):
    cosine, sine_table = angles(SEQ, HD)
    cosine = cosine[:, None, :]
    sine_table = sine_table[:, None, :]
    group_size = HEADS // KVH
    score_scale = 1.0 / math.sqrt(HD)
    positions = jnp.arange(SEQ)

    def forward(tokens, lengths, adapted):
        query_rows = project_rows(tokens, query_weight)
        value_rows = project_rows(tokens, value_weight)
        query_lowrank = project_rows(tokens, query_down).astype(jnp.bfloat16)
        value_lowrank = project_rows(tokens, value_down).astype(jnp.bfloat16)
        if adapted:
            query_rows = query_rows + ADAPTER_SCALE * project_rows(query_lowrank, query_raise_factor)
            value_rows = value_rows + ADAPTER_SCALE * project_rows(value_lowrank, value_raise_factor)
        query_rows = rotate(query_rows.reshape(NSEQ, SEQ, HEADS, HD), cosine, sine_table, 1.0).astype(jnp.bfloat16)
        query_rows = query_rows.reshape(NSEQ, SEQ, KVH, group_size, HD)
        keys_rot = rotate(project_rows(tokens, key_weight).reshape(NSEQ, SEQ, KVH, HD), cosine, sine_table, 1.0).astype(jnp.bfloat16)
        value_rows = value_rows.astype(jnp.bfloat16).reshape(NSEQ, SEQ, KVH, HD)
        scores = jnp.einsum('sqghd,skgd->sghqk', query_rows.astype(jnp.float32), keys_rot.astype(jnp.float32)) * score_scale
        allowed = (positions[None, :] <= positions[:, None])[None] & (positions[None, None, :] < lengths[:, None, None])
        scores = jnp.where(allowed[:, None, None], scores, MASKED)
        row_top = lax.optimization_barrier(jnp.max(scores, axis=-1, keepdims=True))
        exponent = jnp.exp(scores - row_top)
        attention = exponent / lax.optimization_barrier(jnp.sum(exponent, axis=-1, keepdims=True))
        attention_b = attention.astype(jnp.bfloat16)
        context = jnp.einsum('sghqk,skgd->sqghd', attention_b.astype(jnp.float32), value_rows.astype(jnp.float32))
        context = context.astype(jnp.bfloat16).reshape(TOKENS, HEADS * HD)
        return (context, keys_rot, value_rows, attention, attention_b, query_lowrank, value_lowrank)
    reference_context = forward(reference_tokens, reference_lengths, False)[0]
    context, keys_rot, value_rows, attention, attention_b, query_lowrank, value_lowrank = forward(policy_token_inputs, policy_lengths, True)
    pair_sign = (2.0 * chosen_flags.astype(jnp.float32) - 1.0).reshape(NSEQ // 2, 2)
    margin = DPO_BETA * lax.optimization_barrier(jnp.sum(pair_sign * log_ratios.reshape(NSEQ // 2, 2), axis=1))
    seq_scale = (-pair_sign * (DPO_BETA * jax.nn.sigmoid(-margin))[:, None]).reshape(NSEQ)
    live_query = (positions[None, :] < policy_lengths[:, None]).astype(jnp.float32)
    factor = seq_scale[:, None] * live_query
    d_context = (cotangent.astype(jnp.float32).reshape(NSEQ, SEQ, KVH, group_size, HD) * factor[:, :, None, None, None]).astype(jnp.bfloat16)
    d_probs = jnp.einsum('sqghd,skgd->sghqk', d_context.astype(jnp.float32), value_rows.astype(jnp.float32))
    row_total = lax.optimization_barrier(jnp.sum(attention * d_probs, axis=-1, keepdims=True))
    d_scores = (attention * (d_probs - row_total) * score_scale).astype(jnp.bfloat16)
    query_cotangent = jnp.einsum('sghqk,skgd->sqghd', d_scores.astype(jnp.float32), keys_rot.astype(jnp.float32))
    query_cotangent = rotate(query_cotangent.reshape(NSEQ, SEQ, HEADS, HD), cosine, sine_table, -1.0)
    query_cotangent = query_cotangent.reshape(TOKENS, HEADS * HD).astype(jnp.bfloat16)
    value_cotangent = jnp.einsum('sghqk,sqghd->skgd', attention_b.astype(jnp.float32), d_context.astype(jnp.float32))
    value_cotangent = value_cotangent.reshape(TOKENS, KVH * HD).astype(jnp.bfloat16)
    query_up_gradient = ADAPTER_SCALE * jnp.dot(query_lowrank.T, query_cotangent, preferred_element_type=jnp.float32)
    value_up_gradient = ADAPTER_SCALE * jnp.dot(value_lowrank.T, value_cotangent, preferred_element_type=jnp.float32)
    query_input_rows = jnp.dot(query_cotangent, query_raise_factor.T, preferred_element_type=jnp.float32).astype(jnp.bfloat16)
    value_input_rows = jnp.dot(value_cotangent, value_raise_factor.T, preferred_element_type=jnp.float32).astype(jnp.bfloat16)
    query_down_gradient = ADAPTER_SCALE * jnp.dot(policy_token_inputs.T, query_input_rows, preferred_element_type=jnp.float32)
    value_down_gradient = ADAPTER_SCALE * jnp.dot(policy_token_inputs.T, value_input_rows, preferred_element_type=jnp.float32)
    return (reference_context, query_down_gradient, value_down_gradient, query_up_gradient, value_up_gradient)
```

```python
import math

import jax
import jax.numpy as jnp
import numpy as np
from jax import lax
from jax.experimental import pallas as pl
from jax.experimental.pallas import tpu as pltpu
from jax.sharding import PartitionSpec as P

HD = 128
SEQ = 96
TOK = 192
MASKED = -1e30
F32 = jnp.float32
BF16 = jnp.bfloat16
MESH = pl.DeviceIdType.MESH
VM = pl.BlockSpec(memory_space=pltpu.VMEM)
SM = pl.BlockSpec(memory_space=pltpu.SMEM)
NT = 16
NF = 32


def dot(a, b):
    return jnp.dot(a, b, preferred_element_type=F32)


def dot_nt(a, b):
    return lax.dot_general(a, b, (((1,), (1,)), ((), ())), preferred_element_type=F32)


def dot_tn(a, b):
    return lax.dot_general(a, b, (((0,), (0,)), ((), ())), preferred_element_type=F32)


class Place:
    def __init__(self):
        self.f = lax.axis_index("fsdp")
        self.t = lax.axis_index("tensor")
        self.c = lax.rem(self.f, 2)
        self.yh = lax.rem(self.f // 2, 4)
        self.x = self.f // 8
        self.yl = lax.rem(self.t, 2)
        self.z = self.t // 2

    def at(self, x=None, yh=None, c=None, z=None, yl=None):
        x = self.x if x is None else x
        yh = self.yh if yh is None else yh
        c = self.c if c is None else c
        z = self.z if z is None else z
        yl = self.yl if yl is None else yl
        return ((x * 4 + yh) * 2 + c, z * 2 + yl)


class Wires:
    def __init__(self, send, recv):
        self.send, self.recv = send, recv
        self.sent, self.got, self.pending = 0, 0, []

    def slots(self, count):
        base = self.got
        self.got += count
        return base

    def copy(self, src, dst, slot, device, start=True):
        copy = pltpu.make_async_remote_copy(
            src_ref=src,
            dst_ref=dst,
            send_sem=self.send.at[self.sent],
            recv_sem=self.recv.at[slot],
            device_id=device,
            device_id_type=MESH,
        )
        self.sent += 1
        if start:
            copy.start()
            self.pending.append(copy)
        return copy

    def arrived(self, dst, slot, device):
        pltpu.make_async_remote_copy(
            src_ref=dst,
            dst_ref=dst,
            send_sem=self.send.at[0],
            recv_sem=self.recv.at[slot],
            device_id=device,
            device_id_type=MESH,
        ).wait_recv()

    def drain(self):
        for copy in self.pending:
            copy.wait_send()


def greet(devices):
    barrier = pltpu.get_barrier_semaphore()
    for device in devices:
        pl.semaphore_signal(barrier, inc=1, device_id=device, device_id_type=MESH)
    return len(devices)


def met(count):
    pl.semaphore_wait(pltpu.get_barrier_semaphore(), count)


def group_peers(me, axis):
    if axis == "tensor":
        return [(me.f, lax.rem(me.t + d, NT)) for d in range(1, NT)]
    return [(lax.rem(me.f + d, NF), me.t) for d in range(1, NF)]


def scatter_start(wires, me, axis, pieces, landing):
    mine = me.t if axis == "tensor" else me.f
    peers = group_peers(me, axis)
    base = wires.slots(len(peers))
    for d, peer in enumerate(peers):
        to = peer[1] if axis == "tensor" else peer[0]
        wires.copy(pieces.at[to], landing.at[mine], base + d, peer)
    landing[mine] = pieces[mine]
    return base


def scatter_sum(wires, me, axis, landing, base):
    size = NT if axis == "tensor" else NF
    mine = me.t if axis == "tensor" else me.f
    for d in range(1, size):
        source = lax.rem(mine + size - d, size)
        wires.arrived(landing.at[source], base + d - 1, (me.f, me.t))
    total = landing[0]
    for i in range(1, size):
        total = total + landing[i]
    return total


def gather_start(wires, me, axis, blocks):
    mine = me.t if axis == "tensor" else me.f
    peers = group_peers(me, axis)
    base = wires.slots(len(peers))
    for d, peer in enumerate(peers):
        wires.copy(blocks.at[mine], blocks.at[mine], base + d, peer)
    return base


def gather_wait(wires, me, axis, blocks, base):
    size = NT if axis == "tensor" else NF
    mine = me.t if axis == "tensor" else me.f
    for d in range(1, size):
        source = lax.rem(mine + size - d, size)
        wires.arrived(blocks.at[source], base + d - 1, (me.f, me.t))


def project(
    xp, xr, wq, kvx, down, rq,
    qp, kvp, qr, kvr, low, rkv,
    xg, wgq, wgkv, kvt, kvb, flat, lows, lowl, lowg,
    part, sb, rb, ye, send, recv, local,
):
    me = Place()
    c, z, x, yh, yl = me.c, me.z, me.x, me.yh, me.yl
    wires = Wires(send, recv)
    sibling = me.at(c=1 - c)
    ypair = me.at(yl=1 - yl)
    zpair = me.at(z=z + 1 - 2 * lax.rem(z, 2))
    zs = (me.at(z=lax.rem(z + 1, 8)), me.at(z=lax.rem(z + 7, 8)))
    xs = (me.at(x=lax.rem(x + 1, 4)), me.at(x=lax.rem(x + 3, 4)))
    ring = [me.at(yh=lax.rem(yh + d, 4), yl=v) for d in range(1, 4) for v in range(2)]
    count = greet(group_peers(me, "tensor") + [sibling, *xs, *ring])

    def rows(o):
        return pl.ds(pl.multiple_of((c if o == 0 else 1 - c) * TOK, TOK), TOK)

    def features(block):
        return pl.ds(pl.multiple_of(block * 256, 256), 256)

    def xblock(kind, o, zz):
        return xg.at[kind, rows(o), features(zz)]

    def half(ref, which):
        return ref.at[:, features(which)]

    inputs = (xp, xr)
    own = []
    for kind in range(2):
        own.append(pltpu.make_async_copy(half(inputs[kind], c), xblock(kind, 0, z), local.at[kind]))
        own[-1].start()
    met(count)

    yl_d = lax.rem(yh, 2)
    m_own = yh // 2

    def wrows(xx, m):
        return pl.ds(pl.multiple_of((2 * xx + m) * 256, 256), 256)

    def wslot(ref, v, xx, m):
        return ref.at[v, wrows(xx, m)]

    maybe = []

    def y_sends(src, ref, base):
        dst = wslot(ref, yl, x, m_own)
        slot = base + m_own * 2 + yl
        near = wires.copy(src, dst, slot, me.at(yl=yl_d), start=False)
        maybe.append(near)

        @pl.when(yl == yl_d)
        def _():
            pltpu.make_async_copy(src, dst, recv.at[slot]).start()

        @pl.when(yl != yl_d)
        def _():
            near.start()

        for d in (1, 3, 2):
            wires.copy(src, dst, slot, me.at(yh=lax.rem(yh + d, 4), yl=yl_d))

    yq, ykv = wires.slots(4), wires.slots(4)
    y_sends(wq, wgq, yq)
    kz = wires.slots(1)
    wires.copy(kvx, kvt, kz, zpair)
    sib = wires.slots(2)

    def sib_send(kind):
        wires.copy(half(inputs[kind], 1 - c), xblock(kind, 0, z), sib + kind, sibling)

    zbase = wires.slots(2 * 2 * 2 * 4)

    def zidx(kind, o, way, s):
        return zbase + ((kind * 2 + o) * 2 + way) * 4 + s - 1

    def zblock(way, s):
        return lax.rem(z + (8 - s if way == 0 else s), 8)

    def zlast(o, way):
        return 4 if o == way else 3

    def zsend(kind, o, way, s):
        if s > zlast(o, way):
            return
        block = zblock(way, s - 1)
        src = half(inputs[kind], c) if (s == 1 and o == 0) else xblock(kind, o, block)
        wires.copy(src, xblock(kind, o, block), zidx(kind, o, way, s), zs[way])

    def zstep(kind, s):
        for o in range(2):
            for way in range(2):
                if s <= zlast(o, way):
                    wires.arrived(xblock(kind, o, zblock(way, s)), zidx(kind, o, way, s), zs[way])
                    zsend(kind, o, way, s + 1)

    sib_send(0)
    zsend(0, 0, 0, 1)
    zsend(0, 0, 1, 1)
    sib_send(1)

    wires.arrived(kvt, kz, zpair)
    even = lax.rem(z, 2) == 0
    mine, theirs = kvx[...], kvt[...]
    kvb[...] = jnp.where(
        even,
        jnp.concatenate([mine, theirs], axis=1).astype(F32),
        jnp.concatenate([theirs, mine], axis=1).astype(F32),
    ).astype(BF16)
    y_sends(kvb.at[pl.ds(0, 256)], wgkv, ykv)
    ry = wires.slots(1)
    raise_rows = kvb.at[pl.ds(256, 64)]
    wires.copy(raise_rows, rkv.at[yl], ry, ypair)
    rkv[yl] = kvb[pl.ds(256, 64), :]

    wires.arrived(xblock(0, 1, z), sib, sibling)
    zsend(0, 1, 0, 1)
    zsend(0, 1, 1, 1)

    flat[...] = dot(xp[...], down[...])
    for i in range(NT):
        lows[i] = flat[pl.ds(12 * i, 12), :]
    lbase = scatter_start(wires, me, "tensor", lows, lowl)

    xbase = wires.slots(2 * 4 * 2 * 2)
    refs = (wgq, wgkv)
    ybases = (yq, ykv)
    order = [(m_own, yl), (m_own, 1 - yl), (1 - m_own, yl), (1 - m_own, 1 - yl)]

    def xidx(which, j, way, s):
        return xbase + ((which * 4 + j) * 2 + way) * 2 + s - 1

    def xfrom(way, s):
        return lax.rem(x + (4 - s if way == 0 else s), 4)

    def ystep(which, j):
        m, v = order[j]
        block = wslot(refs[which], v, x, m)
        wires.arrived(block, ybases[which] + m * 2 + v, ypair)
        for way in range(2):
            wires.copy(block, block, xidx(which, j, way, 1), xs[way])

    def xwait(which, j, way, s):
        m, v = order[j]
        block = wslot(refs[which], v, xfrom(way, s), m)
        wires.arrived(block, xidx(which, j, way, s), xs[way])
        return block

    def xstep(which, j):
        for way in range(2):
            block = xwait(which, j, way, 1)
            if way == j % 2:
                wires.copy(block, block, xidx(which, j, way, 2), xs[way])

    ystep(0, 0)
    ystep(0, 1)
    zstep(0, 1)
    ystep(1, 0)
    xstep(0, 0)
    ystep(0, 2)
    ystep(1, 1)
    xstep(0, 1)
    zstep(0, 2)
    ystep(0, 3)
    piece = scatter_sum(wires, me, "tensor", lowl, lbase)
    lowg[me.t] = piece
    gbase = gather_start(wires, me, "tensor", lowg)
    for o in range(2):
        if o == 1:
            wires.arrived(xblock(1, 1, z), sib + 1, sibling)
        zsend(1, o, 0, 1)
        zsend(1, o, 1, 1)
    xstep(0, 2)
    ystep(1, 2)
    xstep(1, 0)
    zstep(0, 3)
    xstep(0, 3)
    ystep(1, 3)
    xstep(1, 1)
    zstep(1, 1)
    xstep(1, 2)
    zstep(0, 4)
    xstep(1, 3)
    gather_wait(wires, me, "tensor", lowg, gbase)
    for i in range(NT):
        flat[pl.ds(12 * i, 12), :] = lowg[i]
    low[...] = flat[...].astype(BF16)
    zstep(1, 2)
    for which in range(2):
        for j in range(4):
            xwait(which, j, j % 2, 2)
    for copy in own:
        copy.wait()
    zstep(1, 3)

    pbase, ebase = wires.slots(6), wires.slots(4)

    def partials(kind):
        tokens = xg.at[kind]
        kept = rows(0)
        given = rows(1)
        for g in range(3):
            if g == 0:
                for v in range(2):
                    whole = pl.ds(v * 128, 128)
                    part[kind, g, :, whole] = dot(tokens[kept, :], wgkv[v])
                    sb[kind, g, :, whole] = dot(tokens[given, :], wgkv[v])
            else:
                weight = wgq.at[1 - yl if g == 1 else yl]
                sb[kind, g] = dot(tokens[given, :], weight[...])
                part[kind, g] = dot(tokens[kept, :], weight[...])
            wires.copy(sb.at[kind, g], rb.at[kind, g], pbase + kind * 3 + g, sibling)

    def adapter(cols, matrix):
        return 2.0 * dot(low[:, cols], matrix)

    def exchange(kind):
        for g in range(2):
            wires.arrived(rb.at[kind, g], pbase + kind * 3 + g, sibling)
            part[kind, g] = part[kind, g] + rb[kind, g]
            if kind == 0 and g == 0:
                extra = adapter(pl.ds(64, 64), kvb[pl.ds(256, 64), :])
                for v in range(2):
                    whole = pl.ds(v * 128, 128)
                    part[kind, g, :, whole] = part[kind, g, :, whole] + jnp.where(yl == v, extra, 0.0)
            wires.copy(part.at[kind, g], ye.at[kind, g], ebase + kind * 2 + g, ypair)
        wires.arrived(rb.at[kind, 2], pbase + kind * 3 + 2, sibling)
        part[kind, 2] = part[kind, 2] + rb[kind, 2]

    def finish(kind, query, keyvalue):
        wires.arrived(ye.at[kind, 0], ebase + kind * 2, ypair)
        both = part[kind, 0] + ye[kind, 0]
        keyvalue[0] = both[:, :128]
        keyvalue[1] = both[:, 128:]
        wires.arrived(ye.at[kind, 1], ebase + kind * 2 + 1, ypair)
        total = part[kind, 2] + ye[kind, 1]
        if kind == 0:
            total = total + adapter(pl.ds(0, 64), rq[...])
        query[...] = total

    partials(0)
    zstep(1, 4)
    exchange(0)
    partials(1)
    finish(0, qp, kvp)
    exchange(1)
    finish(1, qr, kvr)
    wires.arrived(rkv.at[1 - yl], ry, ypair)
    for near in maybe:

        @pl.when(yl != yl_d)
        def _(near=near):
            near.wait_send()

    wires.drain()


def lanes(shape):
    return lax.broadcasted_iota(jnp.int32, shape, len(shape) - 1)


def sublanes(shape):
    return lax.broadcasted_iota(jnp.int32, shape, 0)


def key_of(first, second):
    low_half = lax.rem(lanes(first.shape), 64) < 32
    return jnp.where(low_half, first, pltpu.roll(second, 32, axis=1))


def value_of(first, second):
    low_half = lax.rem(lanes(first.shape), 64) < 32
    return jnp.where(low_half, pltpu.roll(first, 96, axis=1), second)


def turned(rows, cosine, sine):
    return rows * cosine + pltpu.roll(rows, 64, axis=1) * sine


def backward(
    xp, cot, rq, qp, kvp, qr, kvr, low, rkv, cosine, sine, plen, rlen, flags, ratios,
    ctx, grad, ups,
    flat, rows_s, rows_l, rows_g, us, ul, upf, ups_s, ups_l, gs, gl, send, recv,
):
    me = Place()
    wires = Wires(send, recv)
    count = greet(group_peers(me, "tensor") + group_peers(me, "fsdp"))
    scale = 1.0 / math.sqrt(HD)
    table_c, table_s = cosine[...], sine[...]
    where_q = lax.rem(sublanes((2 * SEQ, SEQ)), SEQ)
    where_k = lanes((2 * SEQ, SEQ))

    def attend(query, keyvalue, lengths, s):
        at = pl.ds(s * SEQ, SEQ)
        key = turned(key_of(keyvalue[0, at, :], keyvalue[1, at, :]), table_c, table_s).astype(BF16)
        value = value_of(keyvalue[0, at, :], keyvalue[1, at, :]).astype(BF16)
        queries = jnp.concatenate(
            [turned(query[at, pl.ds(h * HD, HD)], table_c, table_s) for h in range(2)], axis=0
        ).astype(BF16)
        scores = dot_nt(queries, key) * scale
        allowed = (where_k <= where_q) & (where_k < lengths[s])
        scores = jnp.where(allowed, scores, MASKED)
        top = jnp.max(scores, axis=1, keepdims=True)
        exponent = jnp.exp(scores - top)
        probs = exponent / jnp.sum(exponent, axis=1, keepdims=True)
        return key, value, probs

    signs = [2.0 * flags[i].astype(F32) - 1.0 for i in range(2)]
    margin = 0.1 * (signs[0] * ratios[0] + signs[1] * ratios[1])
    gate = 0.1 / (1.0 + jnp.exp(jnp.full((SEQ, HD), margin, F32)))
    live = sublanes((SEQ, HD))
    raise_v = value_of(rkv[0].astype(F32), rkv[1].astype(F32)).astype(BF16)
    nothing = jnp.zeros((64, HD), BF16)
    rows_v = jnp.concatenate([nothing, raise_v], axis=0)
    rows_q = [jnp.concatenate([rq[:, pl.ds(h * HD, HD)], nothing], axis=0) for h in range(2)]
    up_q = [jnp.zeros((64, HD), F32) for _ in range(2)]
    up_v = jnp.zeros((64, HD), F32)
    for s in range(2):
        at = pl.ds(s * SEQ, SEQ)
        key, value, probs = attend(qp, kvp, plen, s)
        factor = jnp.where(live < plen[s], -signs[s] * gate, 0.0)
        d_context = jnp.concatenate(
            [cot[at, pl.ds(h * HD, HD)].astype(F32) * factor for h in range(2)], axis=0
        ).astype(BF16)
        d_probs = dot_nt(d_context, value)
        delta = jnp.sum(probs * d_probs, axis=1, keepdims=True)
        d_scores = (probs * (d_probs - delta) * scale).astype(BF16)
        d_query = dot(d_scores, key)
        d_value = dot_tn(probs.astype(BF16), d_context)
        high = d_value.astype(BF16)
        rest = (d_value - high.astype(F32)).astype(BF16)
        lows = low[at, :]
        out = dot_nt(high, rows_v) + dot_nt(rest, rows_v)
        for h in range(2):
            turned_back = turned(d_query[h * SEQ : (h + 1) * SEQ], table_c, -table_s).astype(BF16)
            out = out + dot_nt(turned_back, rows_q[h])
            up_q[h] = up_q[h] + dot_tn(lows, turned_back)[:64]
        up_v = up_v + (dot_tn(lows, high) + dot_tn(lows, rest))[64:]
        flat[at, :] = out
    for i in range(NT):
        rows_s[i] = flat[pl.ds(12 * i, 12), :]
    met(count)
    rbase = scatter_start(wires, me, "tensor", rows_s, rows_l)

    us[...] = up_v
    quarter = lax.rem(me.t, 4)
    first = me.t - quarter
    ubase = wires.slots(3)
    for d in range(1, 4):
        wires.copy(us, ul.at[quarter], ubase + d - 1, (me.f, first + lax.rem(quarter + d, 4)))
    ul[quarter] = up_v

    for s in range(2):
        at = pl.ds(s * SEQ, SEQ)
        key, value, probs = attend(qr, kvr, rlen, s)
        context = dot(probs.astype(BF16), value).astype(BF16)
        for h in range(2):
            ctx[at, pl.ds(h * HD, HD)] = context[h * SEQ : (h + 1) * SEQ]

    piece = scatter_sum(wires, me, "tensor", rows_l, rbase)
    rows_g[me.t] = piece
    gbase = gather_start(wires, me, "tensor", rows_g)
    for d in range(1, 4):
        wires.arrived(ul.at[lax.rem(quarter + 4 - d, 4)], ubase + d - 1, (me.f, me.t))
    upf[pl.ds(0, 64), :] = 2.0 * up_q[0]
    upf[pl.ds(64, 64), :] = 2.0 * up_q[1]
    upf[pl.ds(128, 64), :] = 2.0 * (ul[0] + ul[1] + ul[2] + ul[3])
    for i in range(NF):
        ups_s[i] = upf[pl.ds(6 * i, 6), :]
    upbase = scatter_start(wires, me, "fsdp", ups_s, ups_l)
    gather_wait(wires, me, "tensor", rows_g, gbase)
    for i in range(NT):
        flat[pl.ds(12 * i, 12), :] = rows_g[i]
    down = 2.0 * dot_tn(xp[...], flat[...].astype(BF16))
    gs[...] = down.reshape(NF, 16, 128)
    dbase = scatter_start(wires, me, "fsdp", gs, gl)
    ups[me.f] = scatter_sum(wires, me, "fsdp", ups_l, upbase)
    upgather = gather_start(wires, me, "fsdp", ups)
    grad[me.f] = scatter_sum(wires, me, "fsdp", gl, dbase)
    downgather = gather_start(wires, me, "fsdp", grad)
    gather_wait(wires, me, "fsdp", ups, upgather)
    gather_wait(wires, me, "fsdp", grad, downgather)
    wires.drain()


def tables():
    position = np.arange(SEQ, dtype=np.float32)
    inverse = (500000.0 ** (-(np.arange(HD // 2, dtype=np.float32) * 2.0) / HD)).astype(np.float32)
    phase = (position[:, None] * inverse[None, :]).astype(np.float32)
    cosine, sine = np.cos(phase), np.sin(phase)
    return (
        jnp.asarray(np.concatenate([cosine, cosine], axis=1), F32),
        jnp.asarray(np.concatenate([-sine, sine], axis=1), F32),
    )


def shape(dims, dtype):
    return jax.ShapeDtypeStruct(dims, dtype)


def shards(
    policy_token_inputs,
    reference_tokens,
    cotangent,
    query_weight,
    key_weight,
    value_weight,
    query_down,
    value_down,
    query_raise_factor,
    value_raise_factor,
    policy_lengths,
    reference_lengths,
    chosen_flags,
    log_ratios,
):
    cosine, sine = tables()
    kvx = jnp.concatenate(
        [
            jnp.concatenate([key_weight, value_weight], axis=1),
            jnp.concatenate([jnp.zeros_like(value_raise_factor), value_raise_factor], axis=1),
        ],
        axis=0,
    )
    down = jnp.concatenate([query_down, value_down], axis=1)
    qp, kvp, qr, kvr, low, rkv = pl.pallas_call(
        project,
        out_shape=(
            shape((TOK, 256), F32),
            shape((2, TOK, HD), F32),
            shape((TOK, 256), F32),
            shape((2, TOK, HD), F32),
            shape((TOK, HD), BF16),
            shape((2, 64, HD), BF16),
        ),
        in_specs=[VM] * 6,
        out_specs=(VM,) * 6,
        scratch_shapes=[
            pltpu.VMEM((2, 384, 2048), BF16),
            pltpu.VMEM((2, 2048, 256), BF16),
            pltpu.VMEM((2, 2048, 128), BF16),
            pltpu.VMEM((320, 64), BF16),
            pltpu.VMEM((320, 128), BF16),
            pltpu.VMEM((TOK, 128), F32),
            pltpu.VMEM((NT, 12, 128), F32),
            pltpu.VMEM((NT, 12, 128), F32),
            pltpu.VMEM((NT, 12, 128), F32),
            pltpu.VMEM((2, 3, TOK, 256), F32),
            pltpu.VMEM((2, 3, TOK, 256), F32),
            pltpu.VMEM((2, 3, TOK, 256), F32),
            pltpu.VMEM((2, 2, TOK, 256), F32),
            pltpu.SemaphoreType.DMA((160,)),
            pltpu.SemaphoreType.DMA((160,)),
            pltpu.SemaphoreType.DMA((2,)),
        ],
        compiler_params=pltpu.CompilerParams(collective_id=0, has_side_effects=True),
        name="project",
    )(policy_token_inputs, reference_tokens, query_weight, kvx, down, query_raise_factor)
    context, grad, ups = pl.pallas_call(
        backward,
        out_shape=(
            shape((TOK, 256), BF16),
            shape((NF, 16, 128), F32),
            shape((NF, 6, 128), F32),
        ),
        in_specs=[VM] * 11 + [SM] * 4,
        out_specs=(VM,) * 3,
        scratch_shapes=[
            pltpu.VMEM((TOK, 128), F32),
            pltpu.VMEM((NT, 12, 128), F32),
            pltpu.VMEM((NT, 12, 128), F32),
            pltpu.VMEM((NT, 12, 128), F32),
            pltpu.VMEM((64, 128), F32),
            pltpu.VMEM((4, 64, 128), F32),
            pltpu.VMEM((TOK, 128), F32),
            pltpu.VMEM((NF, 6, 128), F32),
            pltpu.VMEM((NF, 6, 128), F32),
            pltpu.VMEM((NF, 16, 128), F32),
            pltpu.VMEM((NF, 16, 128), F32),
            pltpu.SemaphoreType.DMA((170,)),
            pltpu.SemaphoreType.DMA((170,)),
        ],
        compiler_params=pltpu.CompilerParams(collective_id=1, has_side_effects=True),
        name="backward",
    )(
        policy_token_inputs, cotangent, query_raise_factor, qp, kvp, qr, kvr, low, rkv,
        cosine, sine, policy_lengths, reference_lengths, chosen_flags, log_ratios,
    )
    grad = grad.reshape(512, 128)
    ups = ups.reshape(TOK, 128)
    query_up = jnp.concatenate([ups[:64], ups[64:128]], axis=1)
    piece = lax.rem(lax.axis_index("tensor"), 4)
    value_up = lax.dynamic_slice_in_dim(ups[128:], piece * 32, 32, axis=1)
    return context, grad[:, :64], grad[:, 64:], query_up, value_up


def solution(mesh):
    return jax.shard_map(
        shards,
        mesh=mesh,
        in_specs=(
            P("fsdp", "tensor"),
            P("fsdp", "tensor"),
            P("fsdp", "tensor"),
            P("fsdp", "tensor"),
            P("fsdp", "tensor"),
            P("fsdp", "tensor"),
            P("tensor", None),
            P("tensor", None),
            P(None, "tensor"),
            P(None, "tensor"),
            P("fsdp"),
            P("fsdp"),
            P("fsdp"),
            P("fsdp"),
        ),
        out_specs=(
            P("fsdp", "tensor"),
            P("tensor", None),
            P("tensor", None),
            P(None, "tensor"),
            P(None, "tensor"),
        ),
        check_vma=False,
    )
```

```python
import math

import jax
import jax.numpy as jnp
import numpy as np
from jax import lax
from jax.experimental import pallas as pl
from jax.experimental.pallas import tpu as pltpu
from jax.sharding import PartitionSpec as P

HD = 128
SEQ = 96
TOK = 192
MASKED = -1e30
F32 = jnp.float32
BF16 = jnp.bfloat16
MESH = pl.DeviceIdType.MESH
VM = pl.BlockSpec(memory_space=pltpu.VMEM)
SM = pl.BlockSpec(memory_space=pltpu.SMEM)
NT = 16
NF = 32


def dot(a, b):
    return jnp.dot(a, b, preferred_element_type=F32)


def dot_nt(a, b):
    return lax.dot_general(a, b, (((1,), (1,)), ((), ())), preferred_element_type=F32)


def dot_tn(a, b):
    return lax.dot_general(a, b, (((0,), (0,)), ((), ())), preferred_element_type=F32)


class Place:
    def __init__(self):
        self.f = lax.axis_index("fsdp")
        self.t = lax.axis_index("tensor")
        self.c = lax.rem(self.f, 2)
        self.yh = lax.rem(self.f // 2, 4)
        self.x = self.f // 8
        self.yl = lax.rem(self.t, 2)
        self.z = self.t // 2

    def at(self, x=None, yh=None, c=None, z=None, yl=None):
        x = self.x if x is None else x
        yh = self.yh if yh is None else yh
        c = self.c if c is None else c
        z = self.z if z is None else z
        yl = self.yl if yl is None else yl
        return ((x * 4 + yh) * 2 + c, z * 2 + yl)


class Wires:
    def __init__(self, send, recv):
        self.send, self.recv = send, recv
        self.sent, self.got, self.pending = 0, 0, []

    def slots(self, count):
        base = self.got
        self.got += count
        return base

    def copy(self, src, dst, slot, device, start=True):
        copy = pltpu.make_async_remote_copy(
            src_ref=src,
            dst_ref=dst,
            send_sem=self.send.at[self.sent],
            recv_sem=self.recv.at[slot],
            device_id=device,
            device_id_type=MESH,
        )
        self.sent += 1
        if start:
            copy.start()
            self.pending.append(copy)
        return copy

    def arrived(self, dst, slot, device):
        pltpu.make_async_remote_copy(
            src_ref=dst,
            dst_ref=dst,
            send_sem=self.send.at[0],
            recv_sem=self.recv.at[slot],
            device_id=device,
            device_id_type=MESH,
        ).wait_recv()

    def drain(self):
        for copy in self.pending:
            copy.wait_send()


def greet(devices):
    barrier = pltpu.get_barrier_semaphore()
    for device in devices:
        pl.semaphore_signal(barrier, inc=1, device_id=device, device_id_type=MESH)
    return len(devices)


def met(count):
    pl.semaphore_wait(pltpu.get_barrier_semaphore(), count)


def group_peers(me, axis):
    if axis == "tensor":
        return [(me.f, lax.rem(me.t + d, NT)) for d in range(1, NT)]
    return [(lax.rem(me.f + d, NF), me.t) for d in range(1, NF)]


def scatter_start(wires, me, axis, pieces, landing):
    mine = me.t if axis == "tensor" else me.f
    peers = group_peers(me, axis)
    base = wires.slots(len(peers))
    for d, peer in enumerate(peers):
        to = peer[1] if axis == "tensor" else peer[0]
        wires.copy(pieces.at[to], landing.at[mine], base + d, peer)
    landing[mine] = pieces[mine]
    return base


def scatter_sum(wires, me, axis, landing, base):
    size = NT if axis == "tensor" else NF
    mine = me.t if axis == "tensor" else me.f
    for d in range(1, size):
        source = lax.rem(mine + size - d, size)
        wires.arrived(landing.at[source], base + d - 1, (me.f, me.t))
    total = landing[0].astype(F32)
    for i in range(1, size):
        total = total + landing[i].astype(F32)
    return total


def gather_start(wires, me, axis, blocks):
    mine = me.t if axis == "tensor" else me.f
    peers = group_peers(me, axis)
    base = wires.slots(len(peers))
    for d, peer in enumerate(peers):
        wires.copy(blocks.at[mine], blocks.at[mine], base + d, peer)
    return base


def gather_wait(wires, me, axis, blocks, base):
    size = NT if axis == "tensor" else NF
    mine = me.t if axis == "tensor" else me.f
    for d in range(1, size):
        source = lax.rem(mine + size - d, size)
        wires.arrived(blocks.at[source], base + d - 1, (me.f, me.t))


def lanes(dims):
    return lax.broadcasted_iota(jnp.int32, dims, len(dims) - 1)


def sublanes(dims):
    return lax.broadcasted_iota(jnp.int32, dims, 0)


def turned(rows, cosine, sine):
    return rows * cosine + pltpu.roll(rows, 64, axis=1) * sine


def one_step(
    xp, xr, cot, wq, wkt, wvt, qdt, vdt, rq, rvt, cosine, sine, plen, rlen, flags, ratios,
    ctx, qd_t, vd_t, up_q, up_vt,
    xg, wgq, wgk, kvo, rvx, rvh, low, flat, lows, lowl, lowg,
    kvp, kvs, kvr, kve, kvf, kvz, qpt, qs, qr, qe, query,
    rows_s, rows_l, rows_g, us, ul, upf, ups_s, ups_l, ups, gs, gl, grad, send, recv, local,
):
    me = Place()
    c, z, x, yh, yl = me.c, me.z, me.x, me.yh, me.yl
    wires = Wires(send, recv)
    sibling = me.at(c=1 - c)
    ypair = me.at(yl=1 - yl)
    zpair = me.at(z=z + 1 - 2 * lax.rem(z, 2))
    zs = (me.at(z=lax.rem(z + 1, 8)), me.at(z=lax.rem(z + 7, 8)))
    xs = (me.at(x=lax.rem(x + 1, 4)), me.at(x=lax.rem(x + 3, 4)))
    across = [me.at(yh=lax.rem(yh + d, 4), yl=1 - yl) for d in range(1, 4)]
    count = greet(group_peers(me, "tensor") + group_peers(me, "fsdp") + across)
    quarter = lax.rem(me.t, 4)
    four = me.t - quarter
    quarters = [(me.f, four + lax.rem(quarter + d, 4)) for d in range(1, 4)]

    def rows(o):
        return pl.ds(pl.multiple_of((c if o == 0 else 1 - c) * TOK, TOK), TOK)

    def features(block):
        return pl.ds(pl.multiple_of(block * 256, 256), 256)

    def xblock(kind, o, zz):
        return xg.at[kind, rows(o), features(zz)]

    def half(ref, which):
        return ref.at[:, features(which)]

    inputs = (xp, xr)
    own = []
    for kind in range(2):
        own.append(pltpu.make_async_copy(half(inputs[kind], c), xblock(kind, 0, z), local.at[kind]))
        own[-1].start()

    kvo[pl.ds(0, 32), :] = wkt[...]
    kvo[pl.ds(32, 32), :] = wvt[...]
    rvx[...] = jnp.zeros((128, 64), BF16)
    rvx[pl.ds(pl.multiple_of(yl * 64 + 32, 32), 32), :] = rvt[...]
    my_quarter = pl.ds(pl.multiple_of(quarter * 32, 32), 32)
    rvh[my_quarter, :] = rvt[...]
    down_t = jnp.concatenate([qdt[...], vdt[...]], axis=0)
    flat[...] = dot_nt(xp[...], down_t)
    for i in range(NT):
        lows[i] = flat[pl.ds(12 * i, 12), :]
    met(count)

    yl_d = lax.rem(yh, 2)
    m_own = yh // 2

    def wslot(which, v, xx, m):
        block = features(2 * xx + m)
        if which == 0:
            return wgk.at[pl.ds(pl.multiple_of(v * 64, 64), 64), block]
        return wgq.at[v, block]

    maybe = []

    def y_sends(which, src, base):
        dst = wslot(which, yl, x, m_own)
        slot = base + m_own * 2 + yl
        near = wires.copy(src, dst, slot, me.at(yl=yl_d), start=False)
        maybe.append(near)

        @pl.when(yl == yl_d)
        def _():
            pltpu.make_async_copy(src, dst, recv.at[slot]).start()

        @pl.when(yl != yl_d)
        def _():
            near.start()

        for d in (1, 3, 2):
            wires.copy(src, dst, slot, me.at(yh=lax.rem(yh + d, 4), yl=yl_d))

    ybases = (wires.slots(4), wires.slots(4))
    y_sends(0, kvo, ybases[0])
    sib = wires.slots(2)

    def sib_send(kind):
        wires.copy(half(inputs[kind], 1 - c), xblock(kind, 0, z), sib + kind, sibling)

    zbase = wires.slots(2 * 2 * 2 * 4)

    def zidx(kind, o, way, s):
        return zbase + ((kind * 2 + o) * 2 + way) * 4 + s - 1

    def zblock(way, s):
        return lax.rem(z + (8 - s if way == 0 else s), 8)

    def zlast(o, way):
        return 4 if o == way else 3

    def zsend(kind, o, way, s):
        if s > zlast(o, way):
            return
        block = zblock(way, s - 1)
        src = half(inputs[kind], c) if (s == 1 and o == 0) else xblock(kind, o, block)
        wires.copy(src, xblock(kind, o, block), zidx(kind, o, way, s), zs[way])

    def zstep(kind, s):
        for o in range(2):
            for way in range(2):
                if s <= zlast(o, way):
                    wires.arrived(xblock(kind, o, zblock(way, s)), zidx(kind, o, way, s), zs[way])
                    zsend(kind, o, way, s + 1)

    def zfirst(kind, o):
        if o == 1:
            wires.arrived(xblock(kind, 1, z), sib + kind, sibling)
        zsend(kind, o, 0, 1)
        zsend(kind, o, 1, 1)

    sib_send(0)
    zfirst(0, 0)
    y_sends(1, wq, ybases[1])
    lbase = scatter_start(wires, me, "tensor", lows, lowl)
    vbase = wires.slots(3)
    for d, peer in enumerate(quarters):
        wires.copy(rvt, rvh.at[my_quarter], vbase + d, peer)
    sib_send(1)
    zfirst(0, 1)

    xbase = wires.slots(2 * 4 * 2 * 2)
    orders = (
        [(m_own, yl), (m_own, 1 - yl), (1 - m_own, yl), (1 - m_own, 1 - yl)],
        [(m_own, 1 - yl), (1 - m_own, 1 - yl), (m_own, yl), (1 - m_own, yl)],
    )

    def xidx(which, j, way, s):
        return xbase + ((which * 4 + j) * 2 + way) * 2 + s - 1

    def xfrom(way, s):
        return lax.rem(x + (4 - s if way == 0 else s), 4)

    def ystep(which, j):
        m, v = orders[which][j]
        block = wslot(which, v, x, m)
        wires.arrived(block, ybases[which] + m * 2 + v, ypair)
        for way in range(2):
            wires.copy(block, block, xidx(which, j, way, 1), xs[way])

    def xwait(which, j, way, s):
        m, v = orders[which][j]
        block = wslot(which, v, xfrom(way, s), m)
        wires.arrived(block, xidx(which, j, way, s), xs[way])
        return block

    def xstep(which, j):
        for way in range(2):
            block = xwait(which, j, way, 1)
            if way == j % 2:
                wires.copy(block, block, xidx(which, j, way, 2), xs[way])

    def xend(which, j):
        xwait(which, j, j % 2, 2)

    kbase, qbase = wires.slots(6), wires.slots(6)

    def kv_partial(kind):
        tokens = xg.at[kind]
        kvs[kind] = dot_nt(tokens[rows(1), :], wgk[...])
        wires.copy(kvs.at[kind], kvr.at[kind], kbase + kind * 3, sibling)
        kvp[kind] = dot_nt(tokens[rows(0), :], wgk[...])

    def kv_across(kind):
        wires.arrived(kvr.at[kind], kbase + kind * 3, sibling)
        total = kvp[kind] + kvr[kind]
        if kind == 0:
            total = total + 2.0 * dot_nt(low[:, pl.ds(64, 64)], rvx[...])
        kvp[kind] = total
        wires.copy(kvp.at[kind], kve.at[kind], kbase + kind * 3 + 1, ypair)

    def kv_pieces(kind):
        wires.arrived(kve.at[kind], kbase + kind * 3 + 1, ypair)
        kvf[kind] = kvp[kind] + kve[kind]
        wires.copy(kvf.at[kind], kvz.at[kind], kbase + kind * 3 + 2, zpair)

    def q_partial(kind, g):
        tokens = xg.at[kind]
        weight = wgq.at[1 - yl if g == 0 else yl]
        qs[kind, g] = dot(tokens[rows(1), :], weight[...])
        wires.copy(qs.at[kind, g], qr.at[kind, g], qbase + kind * 3 + g, sibling)
        qpt[kind, g] = dot(tokens[rows(0), :], weight[...])

    def q_across(kind):
        wires.arrived(qr.at[kind, 0], qbase + kind * 3, sibling)
        qpt[kind, 0] = qpt[kind, 0] + qr[kind, 0]
        wires.copy(qpt.at[kind, 0], qe.at[kind], qbase + kind * 3 + 2, ypair)

    def q_final(kind):
        wires.arrived(qr.at[kind, 1], qbase + kind * 3 + 1, sibling)
        wires.arrived(qe.at[kind], qbase + kind * 3 + 2, ypair)
        total = qpt[kind, 1] + qr[kind, 1] + qe[kind]
        if kind == 0:
            total = total + 2.0 * dot(low[:, pl.ds(0, 64)], rq[...])
        query[kind] = total

    scale = 1.0 / math.sqrt(HD)
    table_c, table_s = cosine[...], sine[...]
    where_q = lax.rem(sublanes((2 * SEQ, SEQ)), SEQ)
    where_k = lanes((2 * SEQ, SEQ))
    group = lanes((SEQ, HD)) // 32
    even = lax.rem(z, 2) == 0

    def heads_of(kind, s):
        at = pl.ds(s * SEQ, SEQ)
        mine, theirs = kvf[kind, at, :], kvz[kind, at, :]
        a, b = jnp.where(even, mine, theirs), jnp.where(even, theirs, mine)
        a96, b32 = pltpu.roll(a, 96, axis=1), pltpu.roll(b, 32, axis=1)
        key = jnp.where(group == 0, a, jnp.where(group == 1, a96, jnp.where(group == 2, pltpu.roll(b, 64, axis=1), b32)))
        value = jnp.where(group == 0, a96, jnp.where(group == 1, pltpu.roll(a, 64, axis=1), jnp.where(group == 2, b32, b)))
        return turned(key, table_c, table_s).astype(BF16), value.astype(BF16)

    def attend(kind, key, lengths, s):
        at = pl.ds(s * SEQ, SEQ)
        queries = jnp.concatenate(
            [turned(query[kind, at, pl.ds(h * HD, HD)], table_c, table_s) for h in range(2)], axis=0
        ).astype(BF16)
        scores = dot_nt(queries, key) * scale
        allowed = (where_k <= where_q) & (where_k < lengths[s])
        scores = jnp.where(allowed, scores, MASKED)
        top = jnp.max(scores, axis=1, keepdims=True)
        exponent = jnp.exp(scores - top)
        return exponent / jnp.sum(exponent, axis=1, keepdims=True)

    ystep(0, 0)
    ystep(0, 1)
    ystep(1, 0)
    zstep(0, 1)
    xstep(0, 0)
    xstep(0, 1)
    ystep(0, 2)
    ystep(0, 3)
    ystep(1, 1)
    xstep(0, 2)
    xstep(0, 3)
    zstep(0, 2)
    ystep(1, 2)
    xstep(1, 0)
    piece = scatter_sum(wires, me, "tensor", lowl, lbase)
    lowg[me.t] = piece
    gbase = gather_start(wires, me, "tensor", lowg)
    xstep(1, 1)
    ystep(1, 3)
    zstep(0, 3)
    zfirst(1, 0)
    zfirst(1, 1)
    xstep(1, 2)
    gather_wait(wires, me, "tensor", lowg, gbase)
    for i in range(NT):
        flat[pl.ds(12 * i, 12), :] = lowg[i]
    low[...] = flat[...].astype(BF16)
    zstep(0, 4)
    for copy in own:
        copy.wait()
    for j in range(4):
        xend(0, j)
    kv_partial(0)
    xstep(1, 3)
    zstep(1, 1)
    kv_across(0)
    xend(1, 0)
    xend(1, 1)
    q_partial(0, 0)
    zstep(1, 2)
    kv_pieces(0)
    q_across(0)
    zstep(1, 3)
    xend(1, 2)
    xend(1, 3)
    q_partial(0, 1)
    zstep(1, 4)
    wires.arrived(kvz.at[0], kbase + 2, zpair)
    pair = [heads_of(0, s) for s in range(2)]
    for d in range(1, 4):
        theirs = pl.ds(pl.multiple_of(lax.rem(quarter + 4 - d, 4) * 32, 32), 32)
        wires.arrived(rvh.at[theirs], vbase + d - 1, ypair)
    q_final(0)

    signs = [2.0 * flags[i].astype(F32) - 1.0 for i in range(2)]
    margin = 0.1 * (signs[0] * ratios[0] + signs[1] * ratios[1])
    gate = 0.1 / (1.0 + jnp.exp(jnp.full((SEQ, HD), margin, F32)))
    live = sublanes((SEQ, HD))
    rows_v = jnp.concatenate([jnp.zeros((128, 64), BF16), rvh[...]], axis=1)
    nothing = jnp.zeros((64, HD), BF16)
    rows_q = [jnp.concatenate([rq[:, pl.ds(h * HD, HD)], nothing], axis=0) for h in range(2)]
    grads_q = [[], []]
    grads_v = []
    for s in range(2):
        at = pl.ds(s * SEQ, SEQ)
        key, value = pair[s]
        probs = attend(0, key, plen, s)
        factor = jnp.where(live < plen[s], -signs[s] * gate, 0.0)
        d_context = jnp.concatenate(
            [cot[at, pl.ds(h * HD, HD)].astype(F32) * factor for h in range(2)], axis=0
        ).astype(BF16)
        d_probs = dot_nt(d_context, value)
        delta = jnp.sum(probs * d_probs, axis=1, keepdims=True)
        d_scores = (probs * (d_probs - delta) * scale).astype(BF16)
        d_query = dot(d_scores, key)
        d_value = dot_tn(probs.astype(BF16), d_context)
        high = d_value.astype(BF16)
        rest = (d_value - high.astype(F32)).astype(BF16)
        out = dot(high, rows_v) + dot(rest, rows_v)
        for h in range(2):
            turned_back = turned(d_query[h * SEQ : (h + 1) * SEQ], table_c, -table_s).astype(BF16)
            out = out + dot_nt(turned_back, rows_q[h])
            grads_q[h].append(turned_back)
        grads_v.append((high, rest))
        flat[at, :] = out
    for i in range(NT):
        rows_s[i] = flat[pl.ds(12 * i, 12), :]
    rbase = scatter_start(wires, me, "tensor", rows_s, rows_l)

    lows2 = [low[pl.ds(s * SEQ, SEQ), :] for s in range(2)]
    total_v = sum(dot_tn(part, lows2[s]) for s in range(2) for part in grads_v[s])
    for q in range(4):
        us[q] = 2.0 * total_v[q * 32 : (q + 1) * 32]
    ubase = wires.slots(3)
    for d, peer in enumerate(quarters):
        wires.copy(us.at[lax.rem(quarter + d + 1, 4)], ul.at[quarter], ubase + d, peer)
    ul[quarter] = us[quarter]
    for h in range(2):
        total_q = sum(dot_tn(lows2[s], grads_q[h][s]) for s in range(2))
        upf[pl.ds(h * 64, 64), :] = 2.0 * total_q[:64]

    kv_partial(1)
    q_partial(1, 0)
    rows_g[me.t] = scatter_sum(wires, me, "tensor", rows_l, rbase)
    gbase = gather_start(wires, me, "tensor", rows_g)
    kv_across(1)
    q_across(1)
    q_partial(1, 1)
    for d in range(1, 4):
        wires.arrived(ul.at[lax.rem(quarter + 4 - d, 4)], ubase + d - 1, ypair)
    upf[pl.ds(128, 32), :] = ul[0] + ul[1] + ul[2] + ul[3]
    for i in range(NF):
        ups_s[i] = upf[pl.ds(5 * i, 5), :]
    upbase = scatter_start(wires, me, "fsdp", ups_s, ups_l)
    gather_wait(wires, me, "tensor", rows_g, gbase)
    for i in range(NT):
        flat[pl.ds(12 * i, 12), :] = rows_g[i]
    down = 2.0 * dot_tn(flat[...].astype(BF16), xp[...])
    for i in range(8):
        for j in range(4):
            gs[i * 4 + j] = down[i * 16 : (i + 1) * 16, j * 128 : (j + 1) * 128].astype(BF16)
    dbase = scatter_start(wires, me, "fsdp", gs, gl)
    kv_pieces(1)
    q_final(1)
    ups[me.f] = scatter_sum(wires, me, "fsdp", ups_l, upbase)
    upgather = gather_start(wires, me, "fsdp", ups)
    grad[me.f] = scatter_sum(wires, me, "fsdp", gl, dbase).astype(BF16)
    downgather = gather_start(wires, me, "fsdp", grad)

    wires.arrived(kvz.at[1], kbase + 5, zpair)
    for s in range(2):
        at = pl.ds(s * SEQ, SEQ)
        key, value = heads_of(1, s)
        context = dot(attend(1, key, rlen, s).astype(BF16), value).astype(BF16)
        for h in range(2):
            ctx[at, pl.ds(h * HD, HD)] = context[h * SEQ : (h + 1) * SEQ]

    gather_wait(wires, me, "fsdp", ups, upgather)
    for i in range(NF):
        upf[pl.ds(5 * i, 5), :] = ups[i]
    for h in range(2):
        up_q[:, pl.ds(h * 128, 128)] = upf[pl.ds(h * 64, 64), :]
    up_vt[...] = upf[pl.ds(128, 32), pl.ds(64, 64)]
    gather_wait(wires, me, "fsdp", grad, downgather)
    for i in range(8):
        target = qd_t if i < 4 else vd_t
        for j in range(4):
            target[pl.ds((i % 4) * 16, 16), pl.ds(j * 128, 128)] = grad[i * 4 + j].astype(F32)
    for near in maybe:

        @pl.when(yl != yl_d)
        def _(near=near):
            near.wait_send()

    wires.drain()


def tables():
    position = np.arange(SEQ, dtype=np.float32)
    inverse = (500000.0 ** (-(np.arange(HD // 2, dtype=np.float32) * 2.0) / HD)).astype(np.float32)
    phase = (position[:, None] * inverse[None, :]).astype(np.float32)
    cosine, sine = np.cos(phase), np.sin(phase)
    return (
        jnp.asarray(np.concatenate([cosine, cosine], axis=1), F32),
        jnp.asarray(np.concatenate([-sine, sine], axis=1), F32),
    )


def shape(dims, dtype):
    return jax.ShapeDtypeStruct(dims, dtype)


def shards(
    policy_token_inputs,
    reference_tokens,
    cotangent,
    query_weight,
    key_weight,
    value_weight,
    query_down,
    value_down,
    query_raise_factor,
    value_raise_factor,
    policy_lengths,
    reference_lengths,
    chosen_flags,
    log_ratios,
):
    cosine, sine = tables()
    vm = pltpu.VMEM
    context, qd_t, vd_t, query_up, up_vt = pl.pallas_call(
        one_step,
        out_shape=(
            shape((TOK, 256), BF16),
            shape((64, 512), F32),
            shape((64, 512), F32),
            shape((64, 256), F32),
            shape((32, 64), F32),
        ),
        in_specs=[VM] * 12 + [SM] * 4,
        out_specs=(VM,) * 5,
        scratch_shapes=[
            vm((2, 384, 2048), BF16),
            vm((2, 2048, 256), BF16),
            vm((128, 2048), BF16),
            vm((64, 256), BF16),
            vm((128, 64), BF16),
            vm((128, 64), BF16),
            vm((TOK, 128), BF16),
            vm((TOK, 128), F32),
            vm((NT, 12, 128), F32),
            vm((NT, 12, 128), F32),
            vm((NT, 12, 128), F32),
            *[vm((2, TOK, 128), F32)] * 6,
            *[vm((2, 2, TOK, 256), F32)] * 3,
            *[vm((2, TOK, 256), F32)] * 2,
            *[vm((NT, 12, 128), F32)] * 3,
            *[vm((4, 32, 128), F32)] * 2,
            vm((160, 128), F32),
            *[vm((NF, 5, 128), F32)] * 3,
            *[vm((NF, 16, 128), BF16)] * 3,
            pltpu.SemaphoreType.DMA((300,)),
            pltpu.SemaphoreType.DMA((300,)),
            pltpu.SemaphoreType.DMA((2,)),
        ],
        compiler_params=pltpu.CompilerParams(collective_id=0, has_side_effects=True),
        name="one_step",
    )(
        policy_token_inputs, reference_tokens, cotangent, query_weight, key_weight.T, value_weight.T,
        query_down.T, value_down.T, query_raise_factor, value_raise_factor.T, cosine, sine,
        policy_lengths, reference_lengths, chosen_flags, log_ratios,
    )
    return context, qd_t.T, vd_t.T, query_up, up_vt.T


def solution(mesh):
    return jax.shard_map(
        shards,
        mesh=mesh,
        in_specs=(
            P("fsdp", "tensor"),
            P("fsdp", "tensor"),
            P("fsdp", "tensor"),
            P("fsdp", "tensor"),
            P("fsdp", "tensor"),
            P("fsdp", "tensor"),
            P("tensor", None),
            P("tensor", None),
            P(None, "tensor"),
            P(None, "tensor"),
            P("fsdp"),
            P("fsdp"),
            P("fsdp"),
            P("fsdp"),
        ),
        out_specs=(
            P("fsdp", "tensor"),
            P("tensor", None),
            P("tensor", None),
            P(None, "tensor"),
            P(None, "tensor"),
        ),
        check_vma=False,
    )
```

```python
import math

import jax
import jax.numpy as jnp
import numpy as np
from jax import lax
from jax.experimental import pallas as pl
from jax.experimental.pallas import tpu as pltpu
from jax.sharding import PartitionSpec as P

HD = 128
SEQ = 96
TOK = 192
MASKED = -1e30
F32 = jnp.float32
BF16 = jnp.bfloat16
MESH = pl.DeviceIdType.MESH
VM = pl.BlockSpec(memory_space=pltpu.VMEM)
SM = pl.BlockSpec(memory_space=pltpu.SMEM)
NT = 16
NF = 32


def dot(a, b):
    return jnp.dot(a, b, preferred_element_type=F32)


def dot_nt(a, b):
    return lax.dot_general(a, b, (((1,), (1,)), ((), ())), preferred_element_type=F32)


def dot_tn(a, b):
    return lax.dot_general(a, b, (((0,), (0,)), ((), ())), preferred_element_type=F32)


class Place:
    def __init__(self):
        self.f = lax.axis_index("fsdp")
        self.t = lax.axis_index("tensor")
        self.c = lax.rem(self.f, 2)
        self.yh = lax.rem(self.f // 2, 4)
        self.x = self.f // 8
        self.yl = lax.rem(self.t, 2)
        self.z = self.t // 2

    def at(self, x=None, yh=None, c=None, z=None, yl=None):
        x = self.x if x is None else x
        yh = self.yh if yh is None else yh
        c = self.c if c is None else c
        z = self.z if z is None else z
        yl = self.yl if yl is None else yl
        return ((x * 4 + yh) * 2 + c, z * 2 + yl)


class Wires:
    def __init__(self, send, recv):
        self.send, self.recv = send, recv
        self.sent, self.got, self.pending = 0, 0, []

    def slots(self, count=1):
        base = self.got
        self.got += count
        return base

    def sender(self, everything=None):
        slot = self.sent
        self.sent += 1
        if everything is not None:
            self.pending.append((everything, slot))
        return slot

    def make(self, src, dst, sender, slot, device):
        return pltpu.make_async_remote_copy(
            src_ref=src,
            dst_ref=dst,
            send_sem=self.send.at[sender],
            recv_sem=self.recv.at[slot],
            device_id=device,
            device_id_type=MESH,
        )

    def copy(self, src, dst, slot, device, sender=None):
        sender = self.sender(src) if sender is None else sender
        self.make(src, dst, sender, slot, device).start()

    def arrived(self, dst, slot):
        self.make(dst, dst, 0, slot, self.anyone).wait_recv()

    def left(self, src, sender):
        self.make(src, src, sender, 0, self.anyone).wait_send()

    def drain(self):
        for src, sender in self.pending:
            self.left(src, sender)


def greet(devices):
    barrier = pltpu.get_barrier_semaphore()
    for device in devices:
        pl.semaphore_signal(barrier, inc=1, device_id=device, device_id_type=MESH)
    return len(devices)


def met(count):
    pl.semaphore_wait(pltpu.get_barrier_semaphore(), count)


def group_peers(me, axis):
    if axis == "tensor":
        return [(me.f, lax.rem(me.t + d, NT)) for d in range(1, NT)]
    return [(lax.rem(me.f + d, NF), me.t) for d in range(1, NF)]


def scatter_start(wires, me, axis, pieces, landing):
    mine = me.t if axis == "tensor" else me.f
    peers = group_peers(me, axis)
    slot, sender = wires.slots(), wires.sender(pieces.at[pl.ds(0, len(peers))])
    for peer in peers:
        to = peer[1] if axis == "tensor" else peer[0]
        wires.copy(pieces.at[to], landing.at[mine], slot, peer, sender)
    landing[mine] = pieces[mine]
    return slot


def scatter_sum(wires, axis, landing, slot):
    size = NT if axis == "tensor" else NF
    wires.arrived(landing.at[pl.ds(0, size - 1)], slot)
    total = landing[0].astype(F32)
    for i in range(1, size):
        total = total + landing[i].astype(F32)
    return total


def gather_start(wires, me, axis, blocks):
    mine = me.t if axis == "tensor" else me.f
    peers = group_peers(me, axis)
    slot, sender = wires.slots(), wires.sender(blocks.at[pl.ds(0, len(peers))])
    for peer in peers:
        wires.copy(blocks.at[mine], blocks.at[mine], slot, peer, sender)
    return slot


def gather_wait(wires, axis, blocks, slot):
    size = NT if axis == "tensor" else NF
    wires.arrived(blocks.at[pl.ds(0, size - 1)], slot)


def lanes(dims):
    return lax.broadcasted_iota(jnp.int32, dims, len(dims) - 1)


def sublanes(dims):
    return lax.broadcasted_iota(jnp.int32, dims, 0)


def turned(rows, cosine, sine):
    return rows * cosine + pltpu.roll(rows, 64, axis=1) * sine


def one_step(
    xp, xr, cot, wq, wkt, wvt, qdt, vdt, rq, rvt, cosine, sine, plen, rlen, flags, ratios,
    ctx, qd_t, vd_t, up_q, up_vt,
    xg, wgq, wgk, kvo, rvx, rvh, low, flat, lows, lowl, lowg,
    kvp, kvs, kvr, kve, kvf, kvz, qpt, qs, qr, qe, query,
    rows_s, rows_l, rows_g, us, ul, upf, ups_s, ups_l, ups, gs, gl, grad, send, recv, local,
):
    me = Place()
    c, z, x, yh, yl = me.c, me.z, me.x, me.yh, me.yl
    wires = Wires(send, recv)
    wires.anyone = (me.f, me.t)
    sibling = me.at(c=1 - c)
    ypair = me.at(yl=1 - yl)
    zpair = me.at(z=z + 1 - 2 * lax.rem(z, 2))
    zs = (me.at(z=lax.rem(z + 1, 8)), me.at(z=lax.rem(z + 7, 8)))
    xs = (me.at(x=lax.rem(x + 1, 4)), me.at(x=lax.rem(x + 3, 4)))
    across = [me.at(yh=lax.rem(yh + d, 4), yl=1 - yl) for d in range(1, 4)]
    count = greet(group_peers(me, "tensor") + group_peers(me, "fsdp") + across)
    quarter = lax.rem(me.t, 4)
    four = me.t - quarter
    quarters = [(me.f, four + lax.rem(quarter + d, 4)) for d in range(1, 4)]

    def rows(o):
        return pl.ds(pl.multiple_of((c if o == 0 else 1 - c) * TOK, TOK), TOK)

    def features(block):
        return pl.ds(pl.multiple_of(block * 256, 256), 256)

    def xblock(kind, o, zz):
        return xg.at[kind, rows(o), features(zz)]

    def half(ref, which):
        return ref.at[:, features(which)]

    inputs = (xp, xr)
    own = []
    for kind in range(2):
        own.append(pltpu.make_async_copy(half(inputs[kind], c), xblock(kind, 0, z), local.at[kind]))
        own[-1].start()

    kvo[pl.ds(0, 32), :] = wkt[...]
    kvo[pl.ds(32, 32), :] = wvt[...]
    rvx[...] = jnp.zeros((128, 64), BF16)
    rvx[pl.ds(pl.multiple_of(yl * 64 + 32, 32), 32), :] = rvt[...]
    my_quarter = pl.ds(pl.multiple_of(quarter * 32, 32), 32)
    rvh[my_quarter, :] = rvt[...]
    down_t = jnp.concatenate([qdt[...], vdt[...]], axis=0)
    flat[...] = dot_nt(xp[...], down_t)
    for i in range(NT):
        lows[i] = flat[pl.ds(12 * i, 12), :]
    met(count)

    m_own = yh // 2
    is_inner = 1 - lax.rem(yh + yl, 2)
    inner = is_inner == 1

    def pick(inside, between):
        return is_inner * inside + (1 - is_inner) * between

    up, below = lax.rem(yh + 1, 4), lax.rem(yh + 3, 4)
    partner = me.at(yh=lax.rem(yh + 3 + 2 * lax.rem(yh, 2), 4))
    m_first = pick(m_own, below // 2)

    def wslot(which, v, xx, m):
        block = features(2 * xx + m)
        if which == 0:
            return wgk.at[pl.ds(pl.multiple_of(v * 64, 64), 64), block]
        return wgq.at[v, block]

    def part_of(which, v, xx, m, part):
        block = 2 * xx + m
        if which == 0:
            return wgk.at[pl.ds(pl.multiple_of(v * 64 + part * 32, 32), 32), features(block)]
        return wgq.at[v, pl.ds(pl.multiple_of(block * 256 + part * 128, 128), 128)]

    ybases = (wires.slots(4), wires.slots(4))
    passed = []

    def y_sends(which, src):
        dst = wslot(which, yl, x, m_own)
        near, base = ybases[which], ybases[which] + 2

        stay = pltpu.make_async_copy(src, dst, local.at[2 + which])

        @pl.when(inner)
        def _():
            stay.start()

        to_up = me.at(yh=pick(up, 2 * m_own + 1), yl=pick(yl, 1 - yl))
        to_below = me.at(yh=pick(below, 2 * m_own), yl=pick(yl, 1 - yl))
        wires.copy(src, dst, pick(base, near), to_up)
        wires.copy(src, dst, pick(base + 1, near), to_below)

    def pass_on(which, m, part):
        piece = part_of(which, yl, x, m, part)
        to = me.at(yh=up if part == 0 else below)
        copy = wires.make(piece, piece, wires.sender(), ybases[which] + 2 + part, to)
        passed.append(copy)
        return copy

    def y_arrival(which, j):
        m, v = orders[which][j]
        block = wslot(which, v, x, m)
        base = ybases[which]
        if v is yl:
            first = m is m_first
            if first:
                here = [pltpu.make_async_copy(block, block, local.at[2 + which]).wait]
            else:
                parts = [part_of(which, v, x, m, part) for part in range(2)]
                here = [wires.make(p, p, 0, base + 2 + i, wires.anyone).wait_recv for i, p in enumerate(parts)]
            whole = wires.make(block, block, 0, base + (2 if first else 3), wires.anyone)
            onward = pass_on(which, m, 0 if first else 1)

            @pl.when(inner)
            def _():
                for wait in here:
                    wait()

            @pl.when(jnp.logical_not(inner))
            def _():
                whole.wait_recv()
                onward.start()

        elif m is m_own:
            wires.arrived(block, base)
            wires.copy(block, block, base + 1, partner)
        else:
            wires.arrived(block, base + 1)
        return block

    y_sends(0, kvo)
    sib = wires.slots(2)

    def sib_send(kind):
        wires.copy(half(inputs[kind], 1 - c), xblock(kind, 0, z), sib + kind, sibling)

    zbase = wires.slots(2 * 2 * 2 * 4)

    zsender = wires.sender(xg.at[:, :, pl.ds(0, 7 * 256)])

    def zidx(kind, o, way, s):
        return zbase + ((kind * 2 + o) * 2 + way) * 4 + s - 1

    def zblock(way, s):
        return lax.rem(z + (8 - s if way == 0 else s), 8)

    def zlast(o, way):
        return 4 if o == way else 3

    def zsend(kind, o, way, s):
        if s > zlast(o, way):
            return
        block = zblock(way, s - 1)
        src = half(inputs[kind], c) if (s == 1 and o == 0) else xblock(kind, o, block)
        wires.copy(src, xblock(kind, o, block), zidx(kind, o, way, s), zs[way], zsender)

    def zstep(kind, s):
        for o in range(2):
            for way in range(2):
                if s <= zlast(o, way):
                    wires.arrived(xblock(kind, o, zblock(way, s)), zidx(kind, o, way, s))
                    zsend(kind, o, way, s + 1)

    def zfirst(kind, o):
        if o == 1:
            wires.arrived(xblock(kind, 1, z), sib + kind)
        zsend(kind, o, 0, 1)
        zsend(kind, o, 1, 1)

    sib_send(0)
    zfirst(0, 0)
    y_sends(1, wq)
    lslot = scatter_start(wires, me, "tensor", lows, lowl)
    vslot, vsender = wires.slots(), wires.sender(rvh.at[pl.ds(0, 96)])
    for peer in quarters:
        wires.copy(rvt, rvh.at[my_quarter], vslot, peer, vsender)
    sib_send(1)
    zfirst(0, 1)

    xbase = wires.slots(2 * 4 * 2 * 2)
    xsenders = [wires.sender(ref) for ref in (wgk.at[:, pl.ds(0, 1536)], wgq.at[:, pl.ds(0, 1536)])]
    yo = 1 - yl
    m_other, m_last = 1 - m_own, 1 - m_first
    orders = (
        [(m_own, yo), (m_first, yl), (m_other, yo), (m_last, yl)],
        [(m_own, yo), (m_other, yo), (m_first, yl), (m_last, yl)],
    )

    def xidx(which, j, way, s):
        return xbase + ((which * 4 + j) * 2 + way) * 2 + s - 1

    def xfrom(way, s):
        return lax.rem(x + (4 - s if way == 0 else s), 4)

    def ystep(which, j):
        block = y_arrival(which, j)
        for way in range(2):
            wires.copy(block, block, xidx(which, j, way, 1), xs[way], xsenders[which])

    def xwait(which, j, way, s):
        m, v = orders[which][j]
        block = wslot(which, v, xfrom(way, s), m)
        wires.arrived(block, xidx(which, j, way, s))
        return block

    def xstep(which, j):
        for way in range(2):
            block = xwait(which, j, way, 1)
            if way == j % 2:
                wires.copy(block, block, xidx(which, j, way, 2), xs[way], xsenders[which])

    def xend(which, j):
        xwait(which, j, j % 2, 2)

    kbase, qbase = wires.slots(6), wires.slots(6)

    def kv_partial(kind):
        tokens = xg.at[kind]
        kvs[kind] = dot_nt(tokens[rows(1), :], wgk[...])
        wires.copy(kvs.at[kind], kvr.at[kind], kbase + kind * 3, sibling)
        kvp[kind] = dot_nt(tokens[rows(0), :], wgk[...])

    def kv_across(kind):
        wires.arrived(kvr.at[kind], kbase + kind * 3)
        total = kvp[kind] + kvr[kind]
        if kind == 0:
            total = total + 2.0 * dot_nt(low[:, pl.ds(64, 64)], rvx[...])
        kvp[kind] = total
        wires.copy(kvp.at[kind], kve.at[kind], kbase + kind * 3 + 1, ypair)

    def kv_pieces(kind):
        wires.arrived(kve.at[kind], kbase + kind * 3 + 1)
        kvf[kind] = kvp[kind] + kve[kind]
        wires.copy(kvf.at[kind], kvz.at[kind], kbase + kind * 3 + 2, zpair)

    def q_partial(kind, g):
        tokens = xg.at[kind]
        weight = wgq.at[1 - yl if g == 0 else yl]
        qs[kind, g] = dot(tokens[rows(1), :], weight[...])
        wires.copy(qs.at[kind, g], qr.at[kind, g], qbase + kind * 3 + g, sibling)
        qpt[kind, g] = dot(tokens[rows(0), :], weight[...])

    def q_across(kind):
        wires.arrived(qr.at[kind, 0], qbase + kind * 3)
        qpt[kind, 0] = qpt[kind, 0] + qr[kind, 0]
        wires.copy(qpt.at[kind, 0], qe.at[kind], qbase + kind * 3 + 2, ypair)

    def q_final(kind):
        wires.arrived(qr.at[kind, 1], qbase + kind * 3 + 1)
        wires.arrived(qe.at[kind], qbase + kind * 3 + 2)
        total = qpt[kind, 1] + qr[kind, 1] + qe[kind]
        if kind == 0:
            total = total + 2.0 * dot(low[:, pl.ds(0, 64)], rq[...])
        query[kind] = total

    scale = 1.0 / math.sqrt(HD)
    table_c, table_s = cosine[...], sine[...]
    where_q = lax.rem(sublanes((2 * SEQ, SEQ)), SEQ)
    where_k = lanes((2 * SEQ, SEQ))
    group = lanes((SEQ, HD)) // 32
    even = lax.rem(z, 2) == 0

    def heads_of(kind, s):
        at = pl.ds(s * SEQ, SEQ)
        mine, theirs = kvf[kind, at, :], kvz[kind, at, :]
        a, b = jnp.where(even, mine, theirs), jnp.where(even, theirs, mine)
        a96, b32 = pltpu.roll(a, 96, axis=1), pltpu.roll(b, 32, axis=1)
        key = jnp.where(group == 0, a, jnp.where(group == 1, a96, jnp.where(group == 2, pltpu.roll(b, 64, axis=1), b32)))
        value = jnp.where(group == 0, a96, jnp.where(group == 1, pltpu.roll(a, 64, axis=1), jnp.where(group == 2, b32, b)))
        return turned(key, table_c, table_s).astype(BF16), value.astype(BF16)

    def attend(kind, key, lengths, s):
        at = pl.ds(s * SEQ, SEQ)
        queries = jnp.concatenate(
            [turned(query[kind, at, pl.ds(h * HD, HD)], table_c, table_s) for h in range(2)], axis=0
        ).astype(BF16)
        scores = dot_nt(queries, key) * scale
        allowed = (where_k <= where_q) & (where_k < lengths[s])
        scores = jnp.where(allowed, scores, MASKED)
        top = jnp.max(scores, axis=1, keepdims=True)
        exponent = jnp.exp(scores - top)
        return exponent / jnp.sum(exponent, axis=1, keepdims=True)

    ystep(0, 0)
    ystep(0, 1)
    ystep(1, 0)
    zstep(0, 1)
    xstep(0, 0)
    ystep(0, 2)
    ystep(0, 3)
    xstep(0, 1)
    ystep(1, 1)
    xstep(0, 2)
    xstep(0, 3)
    ystep(1, 2)
    xstep(1, 0)
    zstep(0, 2)
    lowg[me.t] = scatter_sum(wires, "tensor", lowl, lslot)
    gslot = gather_start(wires, me, "tensor", lowg)
    ystep(1, 3)
    xstep(1, 1)
    zstep(0, 3)
    xstep(1, 2)
    zfirst(1, 0)
    zfirst(1, 1)
    gather_wait(wires, "tensor", lowg, gslot)
    for i in range(NT):
        flat[pl.ds(12 * i, 12), :] = lowg[i]
    low[...] = flat[...].astype(BF16)
    zstep(0, 4)
    for copy in own:
        copy.wait()
    for j in range(4):
        xend(0, j)
    kv_partial(0)
    xstep(1, 3)
    kv_across(0)
    xend(1, 0)
    xend(1, 1)
    q_partial(0, 0)
    kv_pieces(0)
    zstep(1, 1)
    q_across(0)
    xend(1, 2)
    xend(1, 3)
    q_partial(0, 1)
    wires.arrived(kvz.at[0], kbase + 2)
    pair = [heads_of(0, s) for s in range(2)]
    wires.arrived(rvh.at[pl.ds(0, 96)], vslot)
    zstep(1, 2)
    q_final(0)

    signs = [2.0 * flags[i].astype(F32) - 1.0 for i in range(2)]
    margin = 0.1 * (signs[0] * ratios[0] + signs[1] * ratios[1])
    gate = 0.1 / (1.0 + jnp.exp(jnp.full((SEQ, HD), margin, F32)))
    live = sublanes((SEQ, HD))
    rows_v = jnp.concatenate([jnp.zeros((128, 64), BF16), rvh[...]], axis=1)
    nothing = jnp.zeros((64, HD), BF16)
    rows_q = [jnp.concatenate([rq[:, pl.ds(h * HD, HD)], nothing], axis=0) for h in range(2)]
    grads_q = [[], []]
    grads_v = []
    for s in range(2):
        at = pl.ds(s * SEQ, SEQ)
        key, value = pair[s]
        probs = attend(0, key, plen, s)
        factor = jnp.where(live < plen[s], -signs[s] * gate, 0.0)
        d_context = jnp.concatenate(
            [cot[at, pl.ds(h * HD, HD)].astype(F32) * factor for h in range(2)], axis=0
        ).astype(BF16)
        d_probs = dot_nt(d_context, value)
        delta = jnp.sum(probs * d_probs, axis=1, keepdims=True)
        d_scores = (probs * (d_probs - delta) * scale).astype(BF16)
        d_query = dot(d_scores, key)
        d_value = dot_tn(probs.astype(BF16), d_context)
        high = d_value.astype(BF16)
        rest = (d_value - high.astype(F32)).astype(BF16)
        out = dot(high, rows_v) + dot(rest, rows_v)
        for h in range(2):
            turned_back = turned(d_query[h * SEQ : (h + 1) * SEQ], table_c, -table_s).astype(BF16)
            out = out + dot_nt(turned_back, rows_q[h])
            grads_q[h].append(turned_back)
        grads_v.append((high, rest))
        flat[at, :] = out
    for i in range(NT):
        rows_s[i] = flat[pl.ds(12 * i, 12), :]
    rbase = scatter_start(wires, me, "tensor", rows_s, rows_l)

    lows2 = [low[pl.ds(s * SEQ, SEQ), :] for s in range(2)]
    total_v = sum(dot_tn(part, lows2[s]) for s in range(2) for part in grads_v[s])
    for q in range(4):
        us[q] = 2.0 * total_v[q * 32 : (q + 1) * 32]
    uslot, usender = wires.slots(), wires.sender(us.at[pl.ds(0, 3)])
    for d, peer in enumerate(quarters):
        wires.copy(us.at[lax.rem(quarter + d + 1, 4)], ul.at[quarter], uslot, peer, usender)
    ul[quarter] = us[quarter]
    for h in range(2):
        total_q = sum(dot_tn(lows2[s], grads_q[h][s]) for s in range(2))
        upf[pl.ds(h * 64, 64), :] = 2.0 * total_q[:64]

    zstep(1, 3)
    rows_g[me.t] = scatter_sum(wires, "tensor", rows_l, rbase)
    gbase = gather_start(wires, me, "tensor", rows_g)
    zstep(1, 4)
    kv_partial(1)
    q_partial(1, 0)
    q_partial(1, 1)
    wires.arrived(ul.at[pl.ds(0, 3)], uslot)
    upf[pl.ds(128, 32), :] = ul[0] + ul[1] + ul[2] + ul[3]
    for i in range(NF):
        ups_s[i] = upf[pl.ds(5 * i, 5), :]
    upbase = scatter_start(wires, me, "fsdp", ups_s, ups_l)
    gather_wait(wires, "tensor", rows_g, gbase)
    for i in range(NT):
        flat[pl.ds(12 * i, 12), :] = rows_g[i]
    down = 2.0 * dot_tn(flat[...].astype(BF16), xp[...])
    for i in range(8):
        for j in range(4):
            gs[i * 4 + j] = down[i * 16 : (i + 1) * 16, j * 128 : (j + 1) * 128].astype(BF16)
    dbase = scatter_start(wires, me, "fsdp", gs, gl)
    kv_across(1)
    q_across(1)
    ups[me.f] = scatter_sum(wires, "fsdp", ups_l, upbase)
    upgather = gather_start(wires, me, "fsdp", ups)
    grad[me.f] = scatter_sum(wires, "fsdp", gl, dbase).astype(BF16)
    downgather = gather_start(wires, me, "fsdp", grad)
    kv_pieces(1)
    q_final(1)

    wires.arrived(kvz.at[1], kbase + 5)
    for s in range(2):
        at = pl.ds(s * SEQ, SEQ)
        key, value = heads_of(1, s)
        context = dot(attend(1, key, rlen, s).astype(BF16), value).astype(BF16)
        for h in range(2):
            ctx[at, pl.ds(h * HD, HD)] = context[h * SEQ : (h + 1) * SEQ]

    gather_wait(wires, "fsdp", ups, upgather)
    for i in range(NF):
        upf[pl.ds(5 * i, 5), :] = ups[i]
    for h in range(2):
        up_q[:, pl.ds(h * 128, 128)] = upf[pl.ds(h * 64, 64), :]
    up_vt[...] = upf[pl.ds(128, 32), pl.ds(64, 64)]
    gather_wait(wires, "fsdp", grad, downgather)
    for i in range(8):
        target = qd_t if i < 4 else vd_t
        for j in range(4):
            target[pl.ds((i % 4) * 16, 16), pl.ds(j * 128, 128)] = grad[i * 4 + j].astype(F32)
    @pl.when(jnp.logical_not(inner))
    def _():
        for copy in passed:
            copy.wait_send()

    wires.drain()
    assert wires.sent <= 64 and wires.got <= 96, (wires.sent, wires.got)


def tables():
    position = np.arange(SEQ, dtype=np.float32)
    inverse = (500000.0 ** (-(np.arange(HD // 2, dtype=np.float32) * 2.0) / HD)).astype(np.float32)
    phase = (position[:, None] * inverse[None, :]).astype(np.float32)
    cosine, sine = np.cos(phase), np.sin(phase)
    return (
        jnp.asarray(np.concatenate([cosine, cosine], axis=1), F32),
        jnp.asarray(np.concatenate([-sine, sine], axis=1), F32),
    )


def shape(dims, dtype):
    return jax.ShapeDtypeStruct(dims, dtype)


def shards(
    policy_token_inputs,
    reference_tokens,
    cotangent,
    query_weight,
    key_weight,
    value_weight,
    query_down,
    value_down,
    query_raise_factor,
    value_raise_factor,
    policy_lengths,
    reference_lengths,
    chosen_flags,
    log_ratios,
):
    cosine, sine = tables()
    vm = pltpu.VMEM
    context, qd_t, vd_t, query_up, up_vt = pl.pallas_call(
        one_step,
        out_shape=(
            shape((TOK, 256), BF16),
            shape((64, 512), F32),
            shape((64, 512), F32),
            shape((64, 256), F32),
            shape((32, 64), F32),
        ),
        in_specs=[VM] * 12 + [SM] * 4,
        out_specs=(VM,) * 5,
        scratch_shapes=[
            vm((2, 384, 2048), BF16),
            vm((2, 2048, 256), BF16),
            vm((128, 2048), BF16),
            vm((64, 256), BF16),
            vm((128, 64), BF16),
            vm((128, 64), BF16),
            vm((TOK, 128), BF16),
            vm((TOK, 128), F32),
            vm((NT, 12, 128), F32),
            vm((NT, 12, 128), F32),
            vm((NT, 12, 128), F32),
            *[vm((2, TOK, 128), F32)] * 6,
            *[vm((2, 2, TOK, 256), F32)] * 3,
            *[vm((2, TOK, 256), F32)] * 2,
            *[vm((NT, 12, 128), F32)] * 3,
            *[vm((4, 32, 128), F32)] * 2,
            vm((160, 128), F32),
            *[vm((NF, 5, 128), F32)] * 3,
            *[vm((NF, 16, 128), BF16)] * 3,
            pltpu.SemaphoreType.DMA((64,)),
            pltpu.SemaphoreType.DMA((96,)),
            pltpu.SemaphoreType.DMA((4,)),
        ],
        compiler_params=pltpu.CompilerParams(collective_id=0, has_side_effects=True),
        name="one_step",
    )(
        policy_token_inputs, reference_tokens, cotangent, query_weight, key_weight.T, value_weight.T,
        query_down.T, value_down.T, query_raise_factor, value_raise_factor.T, cosine, sine,
        policy_lengths, reference_lengths, chosen_flags, log_ratios,
    )
    return context, qd_t.T, vd_t.T, query_up, up_vt.T


def solution(mesh):
    return jax.shard_map(
        shards,
        mesh=mesh,
        in_specs=(
            P("fsdp", "tensor"),
            P("fsdp", "tensor"),
            P("fsdp", "tensor"),
            P("fsdp", "tensor"),
            P("fsdp", "tensor"),
            P("fsdp", "tensor"),
            P("tensor", None),
            P("tensor", None),
            P(None, "tensor"),
            P(None, "tensor"),
            P("fsdp"),
            P("fsdp"),
            P("fsdp"),
            P("fsdp"),
        ),
        out_specs=(
            P("fsdp", "tensor"),
            P("tensor", None),
            P("tensor", None),
            P(None, "tensor"),
            P(None, "tensor"),
        ),
        check_vma=False,
    )
```

```python
import math

import jax
import jax.numpy as jnp
import numpy as np
from jax import lax
from jax.experimental import pallas as pl
from jax.experimental.pallas import tpu as pltpu
from jax.sharding import PartitionSpec as P

HD = 128
SEQ = 96
TOK = 192
MASKED = -1e30
F32 = jnp.float32
BF16 = jnp.bfloat16
MESH = pl.DeviceIdType.MESH
VM = pl.BlockSpec(memory_space=pltpu.VMEM)
SM = pl.BlockSpec(memory_space=pltpu.SMEM)
NT = 16
NF = 32


def dot(a, b):
    return jnp.dot(a, b, preferred_element_type=F32)


def dot_nt(a, b):
    return lax.dot_general(a, b, (((1,), (1,)), ((), ())), preferred_element_type=F32)


def dot_tn(a, b):
    return lax.dot_general(a, b, (((0,), (0,)), ((), ())), preferred_element_type=F32)


class Place:
    def __init__(self):
        self.f = lax.axis_index("fsdp")
        self.t = lax.axis_index("tensor")
        self.c = lax.rem(self.f, 2)
        self.yh = lax.rem(self.f // 2, 4)
        self.x = self.f // 8
        self.yl = lax.rem(self.t, 2)
        self.z = self.t // 2

    def at(self, x=None, yh=None, c=None, z=None, yl=None):
        x = self.x if x is None else x
        yh = self.yh if yh is None else yh
        c = self.c if c is None else c
        z = self.z if z is None else z
        yl = self.yl if yl is None else yl
        return ((x * 4 + yh) * 2 + c, z * 2 + yl)


class Wires:
    def __init__(self, send, recv):
        self.send, self.recv = send, recv
        self.sent, self.got, self.pending = 0, 0, []

    def slots(self, count=1):
        base = self.got
        self.got += count
        return base

    def sender(self, everything=None):
        slot = self.sent
        self.sent += 1
        if everything is not None:
            self.pending.append((everything, slot))
        return slot

    def make(self, src, dst, sender, slot, device):
        return pltpu.make_async_remote_copy(
            src_ref=src,
            dst_ref=dst,
            send_sem=self.send.at[sender],
            recv_sem=self.recv.at[slot],
            device_id=device,
            device_id_type=MESH,
        )

    def copy(self, src, dst, slot, device, sender=None):
        sender = self.sender(src) if sender is None else sender
        self.make(src, dst, sender, slot, device).start()

    def arrived(self, dst, slot):
        self.make(dst, dst, 0, slot, self.anyone).wait_recv()

    def left(self, src, sender):
        self.make(src, src, sender, 0, self.anyone).wait_send()

    def drain(self):
        for src, sender in self.pending:
            self.left(src, sender)


def greet(devices):
    barrier = pltpu.get_barrier_semaphore()
    for device in devices:
        pl.semaphore_signal(barrier, inc=1, device_id=device, device_id_type=MESH)
    return len(devices)


def met(count):
    pl.semaphore_wait(pltpu.get_barrier_semaphore(), count)


def group_peers(me, axis):
    if axis == "tensor":
        return [(me.f, lax.rem(me.t + d, NT)) for d in range(1, NT)]
    return [(lax.rem(me.f + d, NF), me.t) for d in range(1, NF)]


def scatter_start(wires, me, axis, pieces, landing):
    mine = me.t if axis == "tensor" else me.f
    peers = group_peers(me, axis)
    slot, sender = wires.slots(), wires.sender(pieces.at[pl.ds(0, len(peers))])
    for peer in peers:
        to = peer[1] if axis == "tensor" else peer[0]
        wires.copy(pieces.at[to], landing.at[mine], slot, peer, sender)
    landing[mine] = pieces[mine]
    return slot


def scatter_sum(wires, axis, landing, slot):
    size = NT if axis == "tensor" else NF
    wires.arrived(landing.at[pl.ds(0, size - 1)], slot)
    total = landing[0].astype(F32)
    for i in range(1, size):
        total = total + landing[i].astype(F32)
    return total


def gather_start(wires, me, axis, blocks):
    mine = me.t if axis == "tensor" else me.f
    peers = group_peers(me, axis)
    slot, sender = wires.slots(), wires.sender(blocks.at[pl.ds(0, len(peers))])
    for peer in peers:
        wires.copy(blocks.at[mine], blocks.at[mine], slot, peer, sender)
    return slot


def gather_wait(wires, axis, blocks, slot):
    size = NT if axis == "tensor" else NF
    wires.arrived(blocks.at[pl.ds(0, size - 1)], slot)


def lanes(dims):
    return lax.broadcasted_iota(jnp.int32, dims, len(dims) - 1)


def sublanes(dims):
    return lax.broadcasted_iota(jnp.int32, dims, 0)


def turned(rows, cosine, sine):
    return rows * cosine + pltpu.roll(rows, 64, axis=1) * sine


def one_step(
    xp, xr, cot, wq, wkt, wvt, qdt, vdt, rq, rvt, cosine, sine, plen, rlen, flags, ratios,
    ctx, grad, upf,
    xg, wgq, wgk, kvo, rvx, rvh, low, flat, lows, lowl, lowg,
    kvp, kvs, kvr, kve, kvf, kvz, qpt, qs, qr, qe, query,
    rows_s, rows_l, rows_g, us, ul, ups_s, ups_l, ups, gs, gl, send, recv, local,
):
    me = Place()
    c, z, x, yh, yl = me.c, me.z, me.x, me.yh, me.yl
    wires = Wires(send, recv)
    wires.anyone = (me.f, me.t)
    sibling = me.at(c=1 - c)
    ypair = me.at(yl=1 - yl)
    zpair = me.at(z=z + 1 - 2 * lax.rem(z, 2))
    zs = (me.at(z=lax.rem(z + 1, 8)), me.at(z=lax.rem(z + 7, 8)))
    xs = (me.at(x=lax.rem(x + 1, 4)), me.at(x=lax.rem(x + 3, 4)))
    across = [me.at(yh=lax.rem(yh + d, 4), yl=1 - yl) for d in range(1, 4)]
    count = greet(group_peers(me, "tensor") + group_peers(me, "fsdp") + across)
    quarter = lax.rem(me.t, 4)
    four = me.t - quarter
    quarters = [(me.f, four + lax.rem(quarter + d, 4)) for d in range(1, 4)]

    def rows(o):
        return pl.ds(pl.multiple_of((c if o == 0 else 1 - c) * TOK, TOK), TOK)

    def features(block):
        return pl.ds(pl.multiple_of(block * 256, 256), 256)

    def xblock(kind, o, zz):
        return xg.at[kind, rows(o), features(zz)]

    def half(ref, which):
        return ref.at[:, features(which)]

    inputs = (xp, xr)
    own = []
    for kind in range(2):
        own.append(pltpu.make_async_copy(half(inputs[kind], c), xblock(kind, 0, z), local.at[kind]))
        own[-1].start()

    kvo[pl.ds(0, 32), :] = wkt[...]
    kvo[pl.ds(32, 32), :] = wvt[...]
    rvx[...] = jnp.zeros((128, 64), BF16)
    rvx[pl.ds(pl.multiple_of(yl * 64 + 32, 32), 32), :] = rvt[...]
    my_quarter = pl.ds(pl.multiple_of(quarter * 32, 32), 32)
    rvh[my_quarter, :] = rvt[...]
    met(count)

    m_own = yh // 2
    is_inner = 1 - lax.rem(yh + yl, 2)
    inner = is_inner == 1

    def pick(inside, between):
        return is_inner * inside + (1 - is_inner) * between

    up, below = lax.rem(yh + 1, 4), lax.rem(yh + 3, 4)
    partner = me.at(yh=lax.rem(yh + 3 + 2 * lax.rem(yh, 2), 4))
    m_first = pick(m_own, below // 2)

    def wslot(which, v, xx, m):
        block = features(2 * xx + m)
        if which == 0:
            return wgk.at[pl.ds(pl.multiple_of(v * 64, 64), 64), block]
        return wgq.at[v, block]

    def part_of(which, v, xx, m, part):
        block = 2 * xx + m
        if which == 0:
            return wgk.at[pl.ds(pl.multiple_of(v * 64 + part * 32, 32), 32), features(block)]
        return wgq.at[v, pl.ds(pl.multiple_of(block * 256 + part * 128, 128), 128)]

    ybases = (wires.slots(4), wires.slots(4))
    passed = []

    def y_sends(which, src):
        dst = wslot(which, yl, x, m_own)
        near, base = ybases[which], ybases[which] + 2

        stay = pltpu.make_async_copy(src, dst, local.at[2 + which])

        @pl.when(inner)
        def _():
            stay.start()

        to_up = me.at(yh=pick(up, 2 * m_own + 1), yl=pick(yl, 1 - yl))
        to_below = me.at(yh=pick(below, 2 * m_own), yl=pick(yl, 1 - yl))
        wires.copy(src, dst, pick(base, near), to_up)
        wires.copy(src, dst, pick(base + 1, near), to_below)

    def pass_on(which, m, part):
        piece = part_of(which, yl, x, m, part)
        to = me.at(yh=up if part == 0 else below)
        copy = wires.make(piece, piece, wires.sender(), ybases[which] + 2 + part, to)
        passed.append(copy)
        return copy

    def y_arrival(which, j):
        m, v = orders[which][j]
        block = wslot(which, v, x, m)
        base = ybases[which]
        if v is yl:
            first = m is m_first
            if first:
                here = [pltpu.make_async_copy(block, block, local.at[2 + which]).wait]
            else:
                parts = [part_of(which, v, x, m, part) for part in range(2)]
                here = [wires.make(p, p, 0, base + 2 + i, wires.anyone).wait_recv for i, p in enumerate(parts)]
            whole = wires.make(block, block, 0, base + (2 if first else 3), wires.anyone)
            onward = pass_on(which, m, 0 if first else 1)

            @pl.when(inner)
            def _():
                for wait in here:
                    wait()

            @pl.when(jnp.logical_not(inner))
            def _():
                whole.wait_recv()
                onward.start()

        elif m is m_own:
            wires.arrived(block, base)
            wires.copy(block, block, base + 1, partner)
        else:
            wires.arrived(block, base + 1)
        return block

    y_sends(0, kvo)
    sib = wires.slots(2)

    def sib_send(kind):
        wires.copy(half(inputs[kind], 1 - c), xblock(kind, 0, z), sib + kind, sibling)

    zbase = wires.slots(2 * 2 * 2 * 4)

    zsender = wires.sender(xg.at[:, :, pl.ds(0, 7 * 256)])

    def zidx(kind, o, way, s):
        return zbase + ((kind * 2 + o) * 2 + way) * 4 + s - 1

    def zblock(way, s):
        return lax.rem(z + (8 - s if way == 0 else s), 8)

    def zlast(o, way):
        return 4 if o == way else 3

    def zsend(kind, o, way, s):
        if s > zlast(o, way):
            return
        block = zblock(way, s - 1)
        src = half(inputs[kind], c) if (s == 1 and o == 0) else xblock(kind, o, block)
        wires.copy(src, xblock(kind, o, block), zidx(kind, o, way, s), zs[way], zsender)

    def zstep(kind, s):
        for o in range(2):
            for way in range(2):
                if s <= zlast(o, way):
                    wires.arrived(xblock(kind, o, zblock(way, s)), zidx(kind, o, way, s))
                    zsend(kind, o, way, s + 1)

    def zfirst(kind, o):
        if o == 1:
            wires.arrived(xblock(kind, 1, z), sib + kind)
        zsend(kind, o, 0, 1)
        zsend(kind, o, 1, 1)

    sib_send(0)
    zfirst(0, 0)
    y_sends(1, wq)
    down_t = jnp.concatenate([qdt[...], vdt[...]], axis=0)
    flat[...] = dot_nt(xp[...], down_t)
    for i in range(NT):
        lows[i] = flat[pl.ds(12 * i, 12), :]
    lslot = scatter_start(wires, me, "tensor", lows, lowl)
    vslot, vsender = wires.slots(), wires.sender(rvh.at[pl.ds(0, 96)])
    for peer in quarters:
        wires.copy(rvt, rvh.at[my_quarter], vslot, peer, vsender)
    sib_send(1)
    zfirst(0, 1)

    xbase = wires.slots(2 * 4 * 2 * 2)
    xsenders = [wires.sender(ref) for ref in (wgk.at[:, pl.ds(0, 1536)], wgq.at[:, pl.ds(0, 1536)])]
    yo = 1 - yl
    m_other, m_last = 1 - m_own, 1 - m_first
    orders = (
        [(m_own, yo), (m_first, yl), (m_other, yo), (m_last, yl)],
        [(m_own, yo), (m_other, yo), (m_first, yl), (m_last, yl)],
    )

    def xidx(which, j, way, s):
        return xbase + ((which * 4 + j) * 2 + way) * 2 + s - 1

    def xfrom(way, s):
        return lax.rem(x + (4 - s if way == 0 else s), 4)

    def ystep(which, j):
        block = y_arrival(which, j)
        for way in range(2):
            wires.copy(block, block, xidx(which, j, way, 1), xs[way], xsenders[which])

    def xwait(which, j, way, s):
        m, v = orders[which][j]
        block = wslot(which, v, xfrom(way, s), m)
        wires.arrived(block, xidx(which, j, way, s))
        return block

    def xstep(which, j):
        for way in range(2):
            block = xwait(which, j, way, 1)
            if way == j % 2:
                wires.copy(block, block, xidx(which, j, way, 2), xs[way], xsenders[which])

    def xend(which, j):
        xwait(which, j, j % 2, 2)

    kbase, qbase = wires.slots(6), wires.slots(6)

    def kv_partial(kind):
        tokens = xg.at[kind]
        kvs[kind] = dot_nt(tokens[rows(1), :], wgk[...])
        wires.copy(kvs.at[kind], kvr.at[kind], kbase + kind * 3, sibling)
        kvp[kind] = dot_nt(tokens[rows(0), :], wgk[...])

    def kv_across(kind):
        wires.arrived(kvr.at[kind], kbase + kind * 3)
        total = kvp[kind] + kvr[kind]
        if kind == 0:
            total = total + 2.0 * dot_nt(low[:, pl.ds(64, 64)], rvx[...])
        kvp[kind] = total
        wires.copy(kvp.at[kind], kve.at[kind], kbase + kind * 3 + 1, ypair)

    def kv_pieces(kind):
        wires.arrived(kve.at[kind], kbase + kind * 3 + 1)
        kvf[kind] = kvp[kind] + kve[kind]
        wires.copy(kvf.at[kind], kvz.at[kind], kbase + kind * 3 + 2, zpair)

    def q_partial(kind, g):
        tokens = xg.at[kind]
        weight = wgq.at[1 - yl if g == 0 else yl]
        qs[kind, g] = dot(tokens[rows(1), :], weight[...])
        wires.copy(qs.at[kind, g], qr.at[kind, g], qbase + kind * 3 + g, sibling)
        qpt[kind, g] = dot(tokens[rows(0), :], weight[...])

    def q_across(kind):
        wires.arrived(qr.at[kind, 0], qbase + kind * 3)
        qpt[kind, 0] = qpt[kind, 0] + qr[kind, 0]
        wires.copy(qpt.at[kind, 0], qe.at[kind], qbase + kind * 3 + 2, ypair)

    def q_final(kind):
        wires.arrived(qr.at[kind, 1], qbase + kind * 3 + 1)
        wires.arrived(qe.at[kind], qbase + kind * 3 + 2)
        total = qpt[kind, 1] + qr[kind, 1] + qe[kind]
        if kind == 0:
            total = total + 2.0 * dot(low[:, pl.ds(0, 64)], rq[...])
        query[kind] = total

    scale = 1.0 / math.sqrt(HD)
    table_c, table_s = cosine[...], sine[...]
    where_q = lax.rem(sublanes((2 * SEQ, SEQ)), SEQ)
    where_k = lanes((2 * SEQ, SEQ))
    group = lanes((SEQ, HD)) // 32
    even = lax.rem(z, 2) == 0

    def heads_of(kind, s):
        at = pl.ds(s * SEQ, SEQ)
        mine, theirs = kvf[kind, at, :], kvz[kind, at, :]
        a, b = jnp.where(even, mine, theirs), jnp.where(even, theirs, mine)
        a96, b32 = pltpu.roll(a, 96, axis=1), pltpu.roll(b, 32, axis=1)
        key = jnp.where(group == 0, a, jnp.where(group == 1, a96, jnp.where(group == 2, pltpu.roll(b, 64, axis=1), b32)))
        value = jnp.where(group == 0, a96, jnp.where(group == 1, pltpu.roll(a, 64, axis=1), jnp.where(group == 2, b32, b)))
        return turned(key, table_c, table_s).astype(BF16), value.astype(BF16)

    def attend(kind, key, lengths, s):
        at = pl.ds(s * SEQ, SEQ)
        queries = jnp.concatenate(
            [turned(query[kind, at, pl.ds(h * HD, HD)], table_c, table_s) for h in range(2)], axis=0
        ).astype(BF16)
        scores = dot_nt(queries, key) * scale
        allowed = (where_k <= where_q) & (where_k < lengths[s])
        scores = jnp.where(allowed, scores, MASKED)
        top = jnp.max(scores, axis=1, keepdims=True)
        exponent = jnp.exp(scores - top)
        return exponent / jnp.sum(exponent, axis=1, keepdims=True)

    ystep(0, 0)
    ystep(0, 1)
    ystep(1, 0)
    zstep(0, 1)
    xstep(0, 0)
    ystep(0, 2)
    xstep(0, 1)
    ystep(0, 3)
    zfirst(1, 0)
    zfirst(1, 1)
    ystep(1, 1)
    xstep(0, 2)
    xstep(0, 3)
    ystep(1, 2)
    xstep(1, 0)
    zstep(0, 2)
    lowg[me.t] = scatter_sum(wires, "tensor", lowl, lslot)
    gslot = gather_start(wires, me, "tensor", lowg)
    ystep(1, 3)
    xstep(1, 1)
    zstep(0, 3)
    zstep(1, 1)
    xstep(1, 2)
    gather_wait(wires, "tensor", lowg, gslot)
    for i in range(NT):
        flat[pl.ds(12 * i, 12), :] = lowg[i]
    low[...] = flat[...].astype(BF16)
    for j in range(4):
        xend(0, j)
    zstep(0, 4)
    for copy in own:
        copy.wait()
    kv_partial(0)
    xend(1, 0)
    xend(1, 1)
    kv_across(0)
    q_partial(0, 0)
    xstep(1, 3)
    q_across(0)
    zstep(1, 2)
    kv_pieces(0)
    xend(1, 2)
    xend(1, 3)
    q_partial(0, 1)
    zstep(1, 3)
    wires.arrived(kvz.at[0], kbase + 2)
    pair = [heads_of(0, s) for s in range(2)]
    wires.arrived(rvh.at[pl.ds(0, 96)], vslot)
    q_final(0)

    signs = [2.0 * flags[i].astype(F32) - 1.0 for i in range(2)]
    margin = 0.1 * (signs[0] * ratios[0] + signs[1] * ratios[1])
    gate = 0.1 / (1.0 + jnp.exp(jnp.full((SEQ, HD), margin, F32)))
    live = sublanes((SEQ, HD))
    rows_v = jnp.concatenate([jnp.zeros((128, 64), BF16), rvh[...]], axis=1)
    nothing = jnp.zeros((64, HD), BF16)
    rows_q = [jnp.concatenate([rq[:, pl.ds(h * HD, HD)], nothing], axis=0) for h in range(2)]
    grads_q = [[], []]
    grads_v = []
    for s in range(2):
        at = pl.ds(s * SEQ, SEQ)
        key, value = pair[s]
        probs = attend(0, key, plen, s)
        factor = jnp.where(live < plen[s], -signs[s] * gate, 0.0)
        d_context = jnp.concatenate(
            [cot[at, pl.ds(h * HD, HD)].astype(F32) * factor for h in range(2)], axis=0
        ).astype(BF16)
        d_probs = dot_nt(d_context, value)
        delta = jnp.sum(probs * d_probs, axis=1, keepdims=True)
        d_scores = (probs * (d_probs - delta) * scale).astype(BF16)
        d_query = dot(d_scores, key)
        d_value = dot_tn(probs.astype(BF16), d_context)
        high = d_value.astype(BF16)
        rest = (d_value - high.astype(F32)).astype(BF16)
        out = dot(high, rows_v) + dot(rest, rows_v)
        for h in range(2):
            turned_back = turned(d_query[h * SEQ : (h + 1) * SEQ], table_c, -table_s).astype(BF16)
            out = out + dot_nt(turned_back, rows_q[h])
            grads_q[h].append(turned_back)
        grads_v.append((high, rest))
        flat[at, :] = out
    for i in range(NT):
        rows_s[i] = flat[pl.ds(12 * i, 12), :]
    rbase = scatter_start(wires, me, "tensor", rows_s, rows_l)

    lows2 = [low[pl.ds(s * SEQ, SEQ), :] for s in range(2)]
    total_v = sum(dot_tn(part, lows2[s]) for s in range(2) for part in grads_v[s])
    for q in range(4):
        us[q] = 2.0 * total_v[q * 32 : (q + 1) * 32]
    uslot, usender = wires.slots(), wires.sender(us.at[pl.ds(0, 3)])
    for d, peer in enumerate(quarters):
        wires.copy(us.at[lax.rem(quarter + d + 1, 4)], ul.at[quarter], uslot, peer, usender)
    ul[quarter] = us[quarter]
    for h in range(2):
        total_q = sum(dot_tn(lows2[s], grads_q[h][s]) for s in range(2))
        upf[pl.ds(h * 64, 64), :] = 2.0 * total_q[:64]

    rows_g[me.t] = scatter_sum(wires, "tensor", rows_l, rbase)
    gbase = gather_start(wires, me, "tensor", rows_g)
    zstep(1, 4)
    kv_partial(1)
    q_partial(1, 0)
    q_partial(1, 1)
    wires.arrived(ul.at[pl.ds(0, 3)], uslot)
    upf[pl.ds(128, 32), :] = ul[0] + ul[1] + ul[2] + ul[3]
    for i in range(NF):
        ups_s[i] = upf[pl.ds(5 * i, 5), :]
    upbase = scatter_start(wires, me, "fsdp", ups_s, ups_l)
    gather_wait(wires, "tensor", rows_g, gbase)
    for i in range(NT):
        flat[pl.ds(12 * i, 12), :] = rows_g[i]
    down = 2.0 * dot_tn(flat[...].astype(BF16), xp[...])
    for i in range(8):
        for j in range(4):
            gs[i * 4 + j] = down[i * 16 : (i + 1) * 16, j * 128 : (j + 1) * 128].astype(BF16)
    dbase = scatter_start(wires, me, "fsdp", gs, gl)
    kv_across(1)
    q_across(1)
    ups[me.f] = scatter_sum(wires, "fsdp", ups_l, upbase)
    upgather = gather_start(wires, me, "fsdp", ups)
    grad[me.f] = scatter_sum(wires, "fsdp", gl, dbase).astype(BF16)
    downgather = gather_start(wires, me, "fsdp", grad)
    kv_pieces(1)
    q_final(1)

    wires.arrived(kvz.at[1], kbase + 5)
    for s in range(2):
        at = pl.ds(s * SEQ, SEQ)
        key, value = heads_of(1, s)
        context = dot(attend(1, key, rlen, s).astype(BF16), value).astype(BF16)
        for h in range(2):
            ctx[at, pl.ds(h * HD, HD)] = context[h * SEQ : (h + 1) * SEQ]

    gather_wait(wires, "fsdp", ups, upgather)
    for i in range(NF):
        upf[pl.ds(5 * i, 5), :] = ups[i]
    gather_wait(wires, "fsdp", grad, downgather)
    @pl.when(jnp.logical_not(inner))
    def _():
        for copy in passed:
            copy.wait_send()

    wires.drain()
    assert wires.sent <= 64 and wires.got <= 96, (wires.sent, wires.got)


def hand_out(context, grad, ups, ctx, qd_t, vd_t, up_q, up_vt):
    ctx[...] = context[...]
    for i in range(8):
        target = qd_t if i < 4 else vd_t
        for j in range(4):
            target[pl.ds((i % 4) * 16, 16), pl.ds(j * 128, 128)] = grad[i * 4 + j].astype(F32)
    for h in range(2):
        up_q[:, pl.ds(h * 128, 128)] = ups[pl.ds(h * 64, 64), :]
    up_vt[...] = ups[pl.ds(128, 32), pl.ds(64, 64)]


def tables():
    position = np.arange(SEQ, dtype=np.float32)
    inverse = (500000.0 ** (-(np.arange(HD // 2, dtype=np.float32) * 2.0) / HD)).astype(np.float32)
    phase = (position[:, None] * inverse[None, :]).astype(np.float32)
    cosine, sine = np.cos(phase), np.sin(phase)
    return (
        jnp.asarray(np.concatenate([cosine, cosine], axis=1), F32),
        jnp.asarray(np.concatenate([-sine, sine], axis=1), F32),
    )


def shape(dims, dtype):
    return jax.ShapeDtypeStruct(dims, dtype)


def shards(
    policy_token_inputs,
    reference_tokens,
    cotangent,
    query_weight,
    key_weight,
    value_weight,
    query_down,
    value_down,
    query_raise_factor,
    value_raise_factor,
    policy_lengths,
    reference_lengths,
    chosen_flags,
    log_ratios,
):
    cosine, sine = tables()
    vm = pltpu.VMEM
    context, grad, ups = pl.pallas_call(
        one_step,
        out_shape=(
            shape((TOK, 256), BF16),
            shape((NF, 16, 128), BF16),
            shape((160, 128), F32),
        ),
        in_specs=[VM] * 12 + [SM] * 4,
        out_specs=(VM,) * 3,
        scratch_shapes=[
            vm((2, 384, 2048), BF16),
            vm((2, 2048, 256), BF16),
            vm((128, 2048), BF16),
            vm((64, 256), BF16),
            vm((128, 64), BF16),
            vm((128, 64), BF16),
            vm((TOK, 128), BF16),
            vm((TOK, 128), F32),
            vm((NT, 12, 128), F32),
            vm((NT, 12, 128), F32),
            vm((NT, 12, 128), F32),
            *[vm((2, TOK, 128), F32)] * 6,
            *[vm((2, 2, TOK, 256), F32)] * 3,
            *[vm((2, TOK, 256), F32)] * 2,
            *[vm((NT, 12, 128), F32)] * 3,
            *[vm((4, 32, 128), F32)] * 2,
            *[vm((NF, 5, 128), F32)] * 3,
            *[vm((NF, 16, 128), BF16)] * 2,
            pltpu.SemaphoreType.DMA((64,)),
            pltpu.SemaphoreType.DMA((96,)),
            pltpu.SemaphoreType.DMA((4,)),
        ],
        compiler_params=pltpu.CompilerParams(collective_id=0, has_side_effects=True),
        name="one_step",
    )(
        policy_token_inputs, reference_tokens, cotangent, query_weight, key_weight.T, value_weight.T,
        query_down.T, value_down.T, query_raise_factor, value_raise_factor.T, cosine, sine,
        policy_lengths, reference_lengths, chosen_flags, log_ratios,
    )
    context, qd_t, vd_t, query_up, up_vt = pl.pallas_call(
        hand_out,
        out_shape=(
            shape((TOK, 256), BF16),
            shape((64, 512), F32),
            shape((64, 512), F32),
            shape((64, 256), F32),
            shape((32, 64), F32),
        ),
        in_specs=[VM] * 3,
        out_specs=(VM,) * 5,
        name="hand_out",
    )(context, grad, ups)
    return context, qd_t.T, vd_t.T, query_up, up_vt.T


def solution(mesh):
    return jax.shard_map(
        shards,
        mesh=mesh,
        in_specs=(
            P("fsdp", "tensor"),
            P("fsdp", "tensor"),
            P("fsdp", "tensor"),
            P("fsdp", "tensor"),
            P("fsdp", "tensor"),
            P("fsdp", "tensor"),
            P("tensor", None),
            P("tensor", None),
            P(None, "tensor"),
            P(None, "tensor"),
            P("fsdp"),
            P("fsdp"),
            P("fsdp"),
            P("fsdp"),
        ),
        out_specs=(
            P("fsdp", "tensor"),
            P("tensor", None),
            P("tensor", None),
            P(None, "tensor"),
            P(None, "tensor"),
        ),
        check_vma=False,
    )
```

```python
import math

import jax
import jax.numpy as jnp
import numpy as np
from jax import lax
from jax.experimental import pallas as pl
from jax.experimental.pallas import tpu as pltpu
from jax.sharding import PartitionSpec as P

HD = 128
SEQ = 96
TOK = 192
MASKED = -1e30
F32 = jnp.float32
BF16 = jnp.bfloat16
MESH = pl.DeviceIdType.MESH
VM = pl.BlockSpec(memory_space=pltpu.VMEM)
SM = pl.BlockSpec(memory_space=pltpu.SMEM)
NT = 16
NF = 32
SENT = 37
GOT = 96


def dot(a, b):
    return jnp.dot(a, b, preferred_element_type=F32)


def dot_nt(a, b):
    return lax.dot_general(a, b, (((1,), (1,)), ((), ())), preferred_element_type=F32)


def dot_tn(a, b):
    return lax.dot_general(a, b, (((0,), (0,)), ((), ())), preferred_element_type=F32)


class Place:
    def __init__(self):
        self.f = lax.axis_index("fsdp")
        self.t = lax.axis_index("tensor")
        self.c = lax.rem(self.f, 2)
        self.yh = lax.rem(self.f // 2, 4)
        self.x = self.f // 8
        self.yl = lax.rem(self.t, 2)
        self.z = self.t // 2

    def at(self, x=None, yh=None, c=None, z=None, yl=None):
        x = self.x if x is None else x
        yh = self.yh if yh is None else yh
        c = self.c if c is None else c
        z = self.z if z is None else z
        yl = self.yl if yl is None else yl
        return ((x * 4 + yh) * 2 + c, z * 2 + yl)


class Wires:
    def __init__(self, send, recv):
        self.send, self.recv = send, recv
        self.sent, self.got, self.pending = 0, 0, []

    def slots(self, count=1):
        base = self.got
        self.got += count
        return base

    def sender(self, everything=None):
        slot = self.sent
        self.sent += 1
        if everything is not None:
            self.pending.append((everything, slot))
        return slot

    def make(self, src, dst, sender, slot, device):
        return pltpu.make_async_remote_copy(
            src_ref=src,
            dst_ref=dst,
            send_sem=self.send.at[sender],
            recv_sem=self.recv.at[slot],
            device_id=device,
            device_id_type=MESH,
        )

    def copy(self, src, dst, slot, device, sender=None):
        sender = self.sender(src) if sender is None else sender
        self.make(src, dst, sender, slot, device).start()

    def arrived(self, dst, slot):
        self.make(dst, dst, 0, slot, self.anyone).wait_recv()

    def left(self, src, sender):
        self.make(src, src, sender, 0, self.anyone).wait_send()

    def drain(self):
        for src, sender in self.pending:
            self.left(src, sender)


def greet(devices):
    barrier = pltpu.get_barrier_semaphore()
    for device in devices:
        pl.semaphore_signal(barrier, inc=1, device_id=device, device_id_type=MESH)
    return len(devices)


def met(count):
    pl.semaphore_wait(pltpu.get_barrier_semaphore(), count)


def group_peers(me, axis):
    if axis == "tensor":
        return [(me.f, lax.rem(me.t + d, NT)) for d in range(1, NT)]
    return [(lax.rem(me.f + d, NF), me.t) for d in range(1, NF)]


def scatter_start(wires, me, axis, pieces, landing):
    mine = me.t if axis == "tensor" else me.f
    peers = group_peers(me, axis)
    slot, sender = wires.slots(), wires.sender(pieces.at[pl.ds(0, len(peers))])
    for peer in peers:
        to = peer[1] if axis == "tensor" else peer[0]
        wires.copy(pieces.at[to], landing.at[mine], slot, peer, sender)
    landing[mine] = pieces[mine]
    return slot


def scatter_sum(wires, axis, landing, slot):
    size = NT if axis == "tensor" else NF
    wires.arrived(landing.at[pl.ds(0, size - 1)], slot)
    total = landing[0].astype(F32)
    for i in range(1, size):
        total = total + landing[i].astype(F32)
    return total


def gather_start(wires, me, axis, blocks):
    mine = me.t if axis == "tensor" else me.f
    peers = group_peers(me, axis)
    slot, sender = wires.slots(), wires.sender(blocks.at[pl.ds(0, len(peers))])
    for peer in peers:
        wires.copy(blocks.at[mine], blocks.at[mine], slot, peer, sender)
    return slot


def gather_wait(wires, axis, blocks, slot):
    size = NT if axis == "tensor" else NF
    wires.arrived(blocks.at[pl.ds(0, size - 1)], slot)


def lanes(dims):
    return lax.broadcasted_iota(jnp.int32, dims, len(dims) - 1)


def sublanes(dims):
    return lax.broadcasted_iota(jnp.int32, dims, 0)


def turned(rows, cosine, sine):
    return rows * cosine + pltpu.roll(rows, 64, axis=1) * sine


def one_step(
    xp, xr, cot, wq, wkt, wvt, qdt, vdt, rq, rvt, cosine, sine, plen, rlen, flags, ratios,
    ctx, grad, upf,
    xg, wgq, wgk, kvo, rvx, rvh, low, flat, lows, lowl, lowg,
    kvp, kvs, kvr, kve, kvf, kvz, qpt, qs, qr, qe, query,
    rows_s, rows_l, rows_g, us, ul, ups_s, ups_l, ups, gs, gl, send, recv, local,
):
    me = Place()
    c, z, x, yh, yl = me.c, me.z, me.x, me.yh, me.yl
    wires = Wires(send, recv)
    wires.anyone = (me.f, me.t)
    sibling = me.at(c=1 - c)
    ypair = me.at(yl=1 - yl)
    zpair = me.at(z=z + 1 - 2 * lax.rem(z, 2))
    zs = (me.at(z=lax.rem(z + 1, 8)), me.at(z=lax.rem(z + 7, 8)))
    xs = (me.at(x=lax.rem(x + 1, 4)), me.at(x=lax.rem(x + 3, 4)))
    across = [me.at(yh=lax.rem(yh + d, 4), yl=1 - yl) for d in range(1, 4)]
    count = greet(group_peers(me, "tensor") + group_peers(me, "fsdp") + across)
    quarter = lax.rem(me.t, 4)
    four = me.t - quarter
    quarters = [(me.f, four + lax.rem(quarter + d, 4)) for d in range(1, 4)]

    def rows(o):
        return pl.ds(pl.multiple_of((c if o == 0 else 1 - c) * TOK, TOK), TOK)

    def features(block):
        return pl.ds(pl.multiple_of(block * 256, 256), 256)

    def xblock(kind, o, zz):
        return xg.at[kind, rows(o), features(zz)]

    def half(ref, which):
        return ref.at[:, features(which)]

    inputs = (xp, xr)
    own = []
    for kind in range(2):
        own.append(pltpu.make_async_copy(half(inputs[kind], c), xblock(kind, 0, z), local.at[kind]))
        own[-1].start()

    kvo[pl.ds(0, 32), :] = wkt[...]
    kvo[pl.ds(32, 32), :] = wvt[...]
    rvx[...] = jnp.zeros((128, 64), BF16)
    rvx[pl.ds(pl.multiple_of(yl * 64 + 32, 32), 32), :] = rvt[...]
    my_quarter = pl.ds(pl.multiple_of(quarter * 32, 32), 32)
    rvh[my_quarter, :] = rvt[...]
    met(count)

    m_own = yh // 2
    is_inner = 1 - lax.rem(yh + yl, 2)
    inner = is_inner == 1

    def pick(inside, between):
        return is_inner * inside + (1 - is_inner) * between

    up, below = lax.rem(yh + 1, 4), lax.rem(yh + 3, 4)
    partner = me.at(yh=lax.rem(yh + 3 + 2 * lax.rem(yh, 2), 4))
    m_first = pick(m_own, below // 2)

    def wslot(which, v, xx, m):
        block = features(2 * xx + m)
        if which == 0:
            return wgk.at[pl.ds(pl.multiple_of(v * 64, 64), 64), block]
        return wgq.at[v, block]

    def part_of(which, v, xx, m, part):
        block = 2 * xx + m
        if which == 0:
            return wgk.at[pl.ds(pl.multiple_of(v * 64 + part * 32, 32), 32), features(block)]
        return wgq.at[v, pl.ds(pl.multiple_of(block * 256 + part * 128, 128), 128)]

    ybases = (wires.slots(4), wires.slots(4))
    passed = []

    def y_sends(which, src):
        dst = wslot(which, yl, x, m_own)
        near, base = ybases[which], ybases[which] + 2

        stay = pltpu.make_async_copy(src, dst, local.at[2 + which])

        @pl.when(inner)
        def _():
            stay.start()

        to_up = me.at(yh=pick(up, 2 * m_own + 1), yl=pick(yl, 1 - yl))
        to_below = me.at(yh=pick(below, 2 * m_own), yl=pick(yl, 1 - yl))
        wires.copy(src, dst, pick(base, near), to_up)
        wires.copy(src, dst, pick(base + 1, near), to_below)

    def pass_on(which, m, part):
        piece = part_of(which, yl, x, m, part)
        to = me.at(yh=up if part == 0 else below)
        copy = wires.make(piece, piece, wires.sender(), ybases[which] + 2 + part, to)
        passed.append(copy)
        return copy

    def y_arrival(which, j):
        m, v = orders[which][j]
        block = wslot(which, v, x, m)
        base = ybases[which]
        if v is yl:
            first = m is m_first
            if first:
                here = [pltpu.make_async_copy(block, block, local.at[2 + which]).wait]
            else:
                parts = [part_of(which, v, x, m, part) for part in range(2)]
                here = [wires.make(p, p, 0, base + 2 + i, wires.anyone).wait_recv for i, p in enumerate(parts)]
            whole = wires.make(block, block, 0, base + (2 if first else 3), wires.anyone)
            onward = pass_on(which, m, 0 if first else 1)

            @pl.when(inner)
            def _():
                for wait in here:
                    wait()

            @pl.when(jnp.logical_not(inner))
            def _():
                whole.wait_recv()
                onward.start()

        elif m is m_own:
            wires.arrived(block, base)
            wires.copy(block, block, base + 1, partner)
        else:
            wires.arrived(block, base + 1)
        return block

    y_sends(0, kvo)
    sib = wires.slots(2)

    def sib_send(kind):
        wires.copy(half(inputs[kind], 1 - c), xblock(kind, 0, z), sib + kind, sibling)

    zbase = wires.slots(2 * 2 * 2 * 4)

    zsender = wires.sender(xg.at[:, :, pl.ds(0, 7 * 256)])

    def zidx(kind, o, way, s):
        return zbase + ((kind * 2 + o) * 2 + way) * 4 + s - 1

    def zblock(way, s):
        return lax.rem(z + (8 - s if way == 0 else s), 8)

    def zlast(o, way):
        return 4 if o == way else 3

    def zsend(kind, o, way, s):
        if s > zlast(o, way):
            return
        block = zblock(way, s - 1)
        src = half(inputs[kind], c) if (s == 1 and o == 0) else xblock(kind, o, block)
        wires.copy(src, xblock(kind, o, block), zidx(kind, o, way, s), zs[way], zsender)

    def zstep(kind, s):
        for o in range(2):
            for way in range(2):
                if s <= zlast(o, way):
                    wires.arrived(xblock(kind, o, zblock(way, s)), zidx(kind, o, way, s))
                    zsend(kind, o, way, s + 1)

    def zfirst(kind, o):
        if o == 1:
            wires.arrived(xblock(kind, 1, z), sib + kind)
        zsend(kind, o, 0, 1)
        zsend(kind, o, 1, 1)

    sib_send(0)
    zfirst(0, 0)
    y_sends(1, wq)
    down_t = jnp.concatenate([qdt[...], vdt[...]], axis=0)
    flat[...] = dot_nt(xp[...], down_t)
    for i in range(NT):
        lows[i] = flat[pl.ds(12 * i, 12), :]
    lslot = scatter_start(wires, me, "tensor", lows, lowl)
    vslot, vsender = wires.slots(), wires.sender(rvh.at[pl.ds(0, 96)])
    for peer in quarters:
        wires.copy(rvt, rvh.at[my_quarter], vslot, peer, vsender)
    sib_send(1)
    zfirst(0, 1)

    xbase = wires.slots(2 * 4 * 2 * 2)
    xsenders = [wires.sender(ref) for ref in (wgk.at[:, pl.ds(0, 1536)], wgq.at[:, pl.ds(0, 1536)])]
    yo = 1 - yl
    m_other, m_last = 1 - m_own, 1 - m_first
    orders = (
        [(m_own, yo), (m_first, yl), (m_other, yo), (m_last, yl)],
        [(m_own, yo), (m_other, yo), (m_first, yl), (m_last, yl)],
    )

    def xidx(which, j, way, s):
        return xbase + ((which * 4 + j) * 2 + way) * 2 + s - 1

    def xfrom(way, s):
        return lax.rem(x + (4 - s if way == 0 else s), 4)

    def ystep(which, j):
        block = y_arrival(which, j)
        for way in range(2):
            wires.copy(block, block, xidx(which, j, way, 1), xs[way], xsenders[which])

    def xwait(which, j, way, s):
        m, v = orders[which][j]
        block = wslot(which, v, xfrom(way, s), m)
        wires.arrived(block, xidx(which, j, way, s))
        return block

    def xstep(which, j):
        for way in range(2):
            block = xwait(which, j, way, 1)
            if way == j % 2:
                wires.copy(block, block, xidx(which, j, way, 2), xs[way], xsenders[which])

    def xend(which, j):
        xwait(which, j, j % 2, 2)

    kbase, qbase = wires.slots(6), wires.slots(6)

    def kv_partial(kind):
        tokens = xg.at[kind]
        kvs[kind] = dot_nt(tokens[rows(1), :], wgk[...])
        wires.copy(kvs.at[kind], kvr.at[kind], kbase + kind * 3, sibling)
        kvp[kind] = dot_nt(tokens[rows(0), :], wgk[...])

    def kv_across(kind):
        wires.arrived(kvr.at[kind], kbase + kind * 3)
        total = kvp[kind] + kvr[kind]
        if kind == 0:
            total = total + 2.0 * dot_nt(low[:, pl.ds(64, 64)], rvx[...])
        kvp[kind] = total
        wires.copy(kvp.at[kind], kve.at[kind], kbase + kind * 3 + 1, ypair)

    def kv_pieces(kind):
        wires.arrived(kve.at[kind], kbase + kind * 3 + 1)
        kvf[kind] = kvp[kind] + kve[kind]
        wires.copy(kvf.at[kind], kvz.at[kind], kbase + kind * 3 + 2, zpair)

    def q_partial(kind, g):
        tokens = xg.at[kind]
        weight = wgq.at[1 - yl if g == 0 else yl]
        qs[kind, g] = dot(tokens[rows(1), :], weight[...])
        wires.copy(qs.at[kind, g], qr.at[kind, g], qbase + kind * 3 + g, sibling)
        qpt[kind, g] = dot(tokens[rows(0), :], weight[...])

    def q_across(kind):
        wires.arrived(qr.at[kind, 0], qbase + kind * 3)
        qpt[kind, 0] = qpt[kind, 0] + qr[kind, 0]
        wires.copy(qpt.at[kind, 0], qe.at[kind], qbase + kind * 3 + 2, ypair)

    def q_final(kind):
        wires.arrived(qr.at[kind, 1], qbase + kind * 3 + 1)
        wires.arrived(qe.at[kind], qbase + kind * 3 + 2)
        total = qpt[kind, 1] + qr[kind, 1] + qe[kind]
        if kind == 0:
            total = total + 2.0 * dot(low[:, pl.ds(0, 64)], rq[...])
        query[kind] = total

    scale = 1.0 / math.sqrt(HD)
    table_c, table_s = cosine[...], sine[...]
    where_q = lax.rem(sublanes((2 * SEQ, SEQ)), SEQ)
    where_k = lanes((2 * SEQ, SEQ))
    group = lanes((SEQ, HD)) // 32
    even = lax.rem(z, 2) == 0

    def heads_of(kind, s):
        at = pl.ds(s * SEQ, SEQ)
        mine, theirs = kvf[kind, at, :], kvz[kind, at, :]
        a, b = jnp.where(even, mine, theirs), jnp.where(even, theirs, mine)
        a96, b32 = pltpu.roll(a, 96, axis=1), pltpu.roll(b, 32, axis=1)
        key = jnp.where(group == 0, a, jnp.where(group == 1, a96, jnp.where(group == 2, pltpu.roll(b, 64, axis=1), b32)))
        value = jnp.where(group == 0, a96, jnp.where(group == 1, pltpu.roll(a, 64, axis=1), jnp.where(group == 2, b32, b)))
        return turned(key, table_c, table_s).astype(BF16), value.astype(BF16)

    def attend(kind, key, lengths, s):
        at = pl.ds(s * SEQ, SEQ)
        queries = jnp.concatenate(
            [turned(query[kind, at, pl.ds(h * HD, HD)], table_c, table_s) for h in range(2)], axis=0
        ).astype(BF16)
        scores = dot_nt(queries, key) * scale
        allowed = (where_k <= where_q) & (where_k < lengths[s])
        scores = jnp.where(allowed, scores, MASKED)
        top = jnp.max(scores, axis=1, keepdims=True)
        exponent = jnp.exp(scores - top)
        return exponent / jnp.sum(exponent, axis=1, keepdims=True)

    ystep(0, 0)
    ystep(0, 1)
    ystep(1, 0)
    zstep(0, 1)
    xstep(0, 0)
    ystep(0, 2)
    xstep(0, 1)
    ystep(0, 3)
    zfirst(1, 0)
    zfirst(1, 1)
    ystep(1, 1)
    xstep(0, 2)
    xstep(0, 3)
    ystep(1, 2)
    xstep(1, 0)
    zstep(0, 2)
    lowg[me.t] = scatter_sum(wires, "tensor", lowl, lslot)
    gslot = gather_start(wires, me, "tensor", lowg)
    ystep(1, 3)
    xstep(1, 1)
    zstep(0, 3)
    zstep(1, 1)
    xstep(1, 2)
    gather_wait(wires, "tensor", lowg, gslot)
    for i in range(NT):
        flat[pl.ds(12 * i, 12), :] = lowg[i]
    low[...] = flat[...].astype(BF16)
    for j in range(4):
        xend(0, j)
    zstep(0, 4)
    for copy in own:
        copy.wait()
    kv_partial(0)
    xend(1, 0)
    xend(1, 1)
    kv_across(0)
    q_partial(0, 0)
    xstep(1, 3)
    q_across(0)
    zstep(1, 2)
    kv_pieces(0)
    xend(1, 2)
    xend(1, 3)
    q_partial(0, 1)
    zstep(1, 3)
    wires.arrived(kvz.at[0], kbase + 2)
    pair = [heads_of(0, s) for s in range(2)]
    wires.arrived(rvh.at[pl.ds(0, 96)], vslot)
    q_final(0)

    signs = [2.0 * flags[i].astype(F32) - 1.0 for i in range(2)]
    margin = 0.1 * (signs[0] * ratios[0] + signs[1] * ratios[1])
    gate = 0.1 / (1.0 + jnp.exp(jnp.full((SEQ, HD), margin, F32)))
    live = sublanes((SEQ, HD))
    rows_v = jnp.concatenate([jnp.zeros((128, 64), BF16), rvh[...]], axis=1)
    nothing = jnp.zeros((64, HD), BF16)
    rows_q = [jnp.concatenate([rq[:, pl.ds(h * HD, HD)], nothing], axis=0) for h in range(2)]
    grads_q = [[], []]
    grads_v = []
    for s in range(2):
        at = pl.ds(s * SEQ, SEQ)
        key, value = pair[s]
        probs = attend(0, key, plen, s)
        factor = jnp.where(live < plen[s], -signs[s] * gate, 0.0)
        d_context = jnp.concatenate(
            [cot[at, pl.ds(h * HD, HD)].astype(F32) * factor for h in range(2)], axis=0
        ).astype(BF16)
        d_probs = dot_nt(d_context, value)
        delta = jnp.sum(probs * d_probs, axis=1, keepdims=True)
        d_scores = (probs * (d_probs - delta) * scale).astype(BF16)
        d_query = dot(d_scores, key)
        d_value = dot_tn(probs.astype(BF16), d_context)
        high = d_value.astype(BF16)
        rest = (d_value - high.astype(F32)).astype(BF16)
        out = dot(high, rows_v) + dot(rest, rows_v)
        for h in range(2):
            turned_back = turned(d_query[h * SEQ : (h + 1) * SEQ], table_c, -table_s).astype(BF16)
            out = out + dot_nt(turned_back, rows_q[h])
            grads_q[h].append(turned_back)
        grads_v.append((high, rest))
        flat[at, :] = out
    for i in range(NT):
        rows_s[i] = flat[pl.ds(12 * i, 12), :]
    rbase = scatter_start(wires, me, "tensor", rows_s, rows_l)

    lows2 = [low[pl.ds(s * SEQ, SEQ), :] for s in range(2)]
    total_v = sum(dot_tn(part, lows2[s]) for s in range(2) for part in grads_v[s])
    for q in range(4):
        us[q] = 2.0 * total_v[q * 32 : (q + 1) * 32]
    uslot, usender = wires.slots(), wires.sender(us.at[pl.ds(0, 3)])
    for d, peer in enumerate(quarters):
        wires.copy(us.at[lax.rem(quarter + d + 1, 4)], ul.at[quarter], uslot, peer, usender)
    ul[quarter] = us[quarter]
    for h in range(2):
        total_q = sum(dot_tn(lows2[s], grads_q[h][s]) for s in range(2))
        upf[pl.ds(h * 64, 64), :] = 2.0 * total_q[:64]

    rows_g[me.t] = scatter_sum(wires, "tensor", rows_l, rbase)
    gbase = gather_start(wires, me, "tensor", rows_g)
    zstep(1, 4)
    kv_partial(1)
    q_partial(1, 0)
    q_partial(1, 1)
    wires.arrived(ul.at[pl.ds(0, 3)], uslot)
    upf[pl.ds(128, 32), :] = ul[0] + ul[1] + ul[2] + ul[3]
    for i in range(NF):
        ups_s[i] = upf[pl.ds(5 * i, 5), :]
    upbase = scatter_start(wires, me, "fsdp", ups_s, ups_l)
    gather_wait(wires, "tensor", rows_g, gbase)
    for i in range(NT):
        flat[pl.ds(12 * i, 12), :] = rows_g[i]
    down = 2.0 * dot_tn(flat[...].astype(BF16), xp[...])
    for i in range(8):
        for j in range(4):
            gs[i * 4 + j] = down[i * 16 : (i + 1) * 16, j * 128 : (j + 1) * 128].astype(BF16)
    dbase = scatter_start(wires, me, "fsdp", gs, gl)
    kv_across(1)
    q_across(1)
    ups[me.f] = scatter_sum(wires, "fsdp", ups_l, upbase)
    upgather = gather_start(wires, me, "fsdp", ups)
    grad[me.f] = scatter_sum(wires, "fsdp", gl, dbase).astype(BF16)
    downgather = gather_start(wires, me, "fsdp", grad)
    kv_pieces(1)
    q_final(1)

    wires.arrived(kvz.at[1], kbase + 5)
    for s in range(2):
        at = pl.ds(s * SEQ, SEQ)
        key, value = heads_of(1, s)
        context = dot(attend(1, key, rlen, s).astype(BF16), value).astype(BF16)
        for h in range(2):
            ctx[at, pl.ds(h * HD, HD)] = context[h * SEQ : (h + 1) * SEQ]

    gather_wait(wires, "fsdp", ups, upgather)
    for i in range(NF):
        upf[pl.ds(5 * i, 5), :] = ups[i]
    gather_wait(wires, "fsdp", grad, downgather)
    @pl.when(jnp.logical_not(inner))
    def _():
        for copy in passed:
            copy.wait_send()

    wires.drain()
    assert (wires.sent, wires.got) == (SENT, GOT), (wires.sent, wires.got)


def hand_out(context, grad, ups, ctx, qd_t, vd_t, up_q, up_vt):
    ctx[...] = context[...]
    for i in range(8):
        target = qd_t if i < 4 else vd_t
        for j in range(4):
            target[pl.ds((i % 4) * 16, 16), pl.ds(j * 128, 128)] = grad[i * 4 + j].astype(F32)
    for h in range(2):
        up_q[:, pl.ds(h * 128, 128)] = ups[pl.ds(h * 64, 64), :]
    up_vt[...] = ups[pl.ds(128, 32), pl.ds(64, 64)]


def tables():
    position = np.arange(SEQ, dtype=np.float32)
    inverse = (500000.0 ** (-(np.arange(HD // 2, dtype=np.float32) * 2.0) / HD)).astype(np.float32)
    phase = (position[:, None] * inverse[None, :]).astype(np.float32)
    cosine, sine = np.cos(phase), np.sin(phase)
    return (
        jnp.asarray(np.concatenate([cosine, cosine], axis=1), F32),
        jnp.asarray(np.concatenate([-sine, sine], axis=1), F32),
    )


def shape(dims, dtype):
    return jax.ShapeDtypeStruct(dims, dtype)


def shards(
    policy_token_inputs,
    reference_tokens,
    cotangent,
    query_weight,
    key_weight,
    value_weight,
    query_down,
    value_down,
    query_raise_factor,
    value_raise_factor,
    policy_lengths,
    reference_lengths,
    chosen_flags,
    log_ratios,
):
    cosine, sine = tables()
    vm = pltpu.VMEM
    context, grad, ups = pl.pallas_call(
        one_step,
        out_shape=(
            shape((TOK, 256), BF16),
            shape((NF, 16, 128), BF16),
            shape((160, 128), F32),
        ),
        in_specs=[VM] * 12 + [SM] * 4,
        out_specs=(VM,) * 3,
        scratch_shapes=[
            vm((2, 384, 2048), BF16),
            vm((2, 2048, 256), BF16),
            vm((128, 2048), BF16),
            vm((64, 256), BF16),
            vm((128, 64), BF16),
            vm((128, 64), BF16),
            vm((TOK, 128), BF16),
            vm((TOK, 128), F32),
            vm((NT, 12, 128), F32),
            vm((NT, 12, 128), F32),
            vm((NT, 12, 128), F32),
            *[vm((2, TOK, 128), F32)] * 6,
            *[vm((2, 2, TOK, 256), F32)] * 3,
            *[vm((2, TOK, 256), F32)] * 2,
            *[vm((NT, 12, 128), F32)] * 3,
            *[vm((4, 32, 128), F32)] * 2,
            *[vm((NF, 5, 128), F32)] * 3,
            *[vm((NF, 16, 128), BF16)] * 2,
            pltpu.SemaphoreType.DMA((SENT,)),
            pltpu.SemaphoreType.DMA((GOT,)),
            pltpu.SemaphoreType.DMA((4,)),
        ],
        compiler_params=pltpu.CompilerParams(collective_id=0, has_side_effects=True),
        name="one_step",
    )(
        policy_token_inputs, reference_tokens, cotangent, query_weight, key_weight.T, value_weight.T,
        query_down.T, value_down.T, query_raise_factor, value_raise_factor.T, cosine, sine,
        policy_lengths, reference_lengths, chosen_flags, log_ratios,
    )
    context, qd_t, vd_t, query_up, up_vt = pl.pallas_call(
        hand_out,
        out_shape=(
            shape((TOK, 256), BF16),
            shape((64, 512), F32),
            shape((64, 512), F32),
            shape((64, 256), F32),
            shape((32, 64), F32),
        ),
        in_specs=[VM] * 3,
        out_specs=(VM,) * 5,
        name="hand_out",
    )(context, grad, ups)
    return context, qd_t.T, vd_t.T, query_up, up_vt.T


def solution(mesh):
    return jax.shard_map(
        shards,
        mesh=mesh,
        in_specs=(
            P("fsdp", "tensor"),
            P("fsdp", "tensor"),
            P("fsdp", "tensor"),
            P("fsdp", "tensor"),
            P("fsdp", "tensor"),
            P("fsdp", "tensor"),
            P("tensor", None),
            P("tensor", None),
            P(None, "tensor"),
            P(None, "tensor"),
            P("fsdp"),
            P("fsdp"),
            P("fsdp"),
            P("fsdp"),
        ),
        out_specs=(
            P("fsdp", "tensor"),
            P("tensor", None),
            P("tensor", None),
            P(None, "tensor"),
            P(None, "tensor"),
        ),
        check_vma=False,
    )
```
